128 devices in a mesh: tm: 8 (over x, core), rows: 16 (over z, y).
Axes of the slice: x: 4, y: 4, z: 4, core: 2. Of those that a mesh axis runs over, the one named last changes fastest.
Arguments:
- features: bfloat16 [16, 32, 128, 384], P('tm', 'rows'), may hold values from -6 to 6
- block_gain: float32 [384], replicated, may hold values from 0.5 to 1.5
- conv_weight: bfloat16 [3, 3, 3, 384, 384], replicated, may hold values from -0.0625 to 0.0625
- conv_bias: float32 [384], replicated, may hold values from -3 to 3
- latent_weight: bfloat16 [384, 16], replicated, may hold values from -0.3125 to 0.3125
- latent_bias: float32 [16], replicated, may hold values from -3 to 3
- patch_weight: bfloat16 [64, 5120], replicated, may hold values from -0.75 to 0.75
- patch_bias: float32 [5120], replicated, may hold values from -3 to 3
- shift_mod: float32 [5120], replicated, may hold values from -4 to 4
- scale_mod: float32 [5120], replicated, may hold values from -2 to 2
- query_weight: bfloat16 [5120, 5120], P(None, 'tm'), may hold values from -0.078125 to 0.078125
- query_bias: float32 [5120], P('tm'), may hold values from -4 to 4
- query_gain: float32 [5120], P('tm'), may hold values from 0.5 to 1.5
- key_weight: bfloat16 [5120, 5120], P(None, 'tm'), may hold values from -0.078125 to 0.078125
- key_bias: float32 [5120], P('tm'), may hold values from -4 to 4
- key_gain: float32 [5120], P('tm'), may hold values from 0.5 to 1.5
- packing: int32 [128], replicated, may hold values from 0 to 127, each once
Outputs:
- queries: bfloat16 [16384, 5120], P('rows', 'tm')
- keys: bfloat16 [16384, 5120], P('rows', 'tm')
The draws below stay inside these ranges and needn't reach their ends.
All inputs are finite; a program needn't handle non-finite values.
Results may differ from the reference program's by a relative error of at most 0.0054.
Values may be sent and summed in bfloat16 or wider, within the bound.
No kernel may reach another device: no remote copies, remote signals or barrier semaphores. Data moves between devices by JAX's collectives and lax.ppermute only.
A program may use at most 128 MiB of HBM per device.

```python
import jax
import jax.numpy as jnp
from jax import lax

C = 384
LAT = 16
D = 5120
FR_DEV = 2
ROW_DEV = 2
COLS = 128
TOK_DEV = 128
FRAMES = 16
ROWS_ALL = 32
BLOCKS = 128
TOKENS = 16384
N_TM = 8
N_ROWS = 16


def level_of(own_key, shape, shards, smallest, top_value):
    level, own = 1.0, jax.random.fold_in(own_key, 6)
    for axis_at, parts in shards:
        heights = jnp.exp(jax.random.uniform(jax.random.fold_in(own, axis_at), (parts,), jnp.float32, smallest / len(shards), top_value / len(shards)))
        level = level * jnp.repeat(heights, shape[axis_at] // parts).reshape([-1 if axis == axis_at else 1 for axis in range(len(shape))])
    return level


def noise(rng, extent, deviation, limit, cuts=(), kind=jnp.bfloat16):
    values = deviation * jax.random.normal(rng, extent, jnp.float32)
    if cuts:
        values = values * level_of(rng, extent, cuts, -0.22, 0.18)
    return jnp.clip(values, -limit, limit).astype(kind)


def setup_inputs(seed: int = 0) -> dict:
    seeds = jax.random.split(jax.random.key(seed), 18)
    return {
        "features": noise(seeds[0], (FRAMES, ROWS_ALL, COLS, C), 1.0, 6.0, ((0, 8), (1, 16))),
        "block_gain": jnp.clip(jax.random.uniform(seeds[1], (C,), jnp.float32, 0.5, 1.5), 0.5, 1.5),
        "conv_weight": noise(seeds[2], (3, 3, 3, C, C), (27 * C) ** -0.5, 0.0625),
        "conv_bias": noise(seeds[3], (C,), 0.5, 3.0, (), jnp.float32),
        "latent_weight": noise(seeds[4], (C, LAT), C ** -0.5, 0.3125),
        "latent_bias": noise(seeds[5], (LAT,), 0.5, 3.0, (), jnp.float32),
        "patch_weight": noise(seeds[6], (4 * LAT, D), (4 * LAT) ** -0.5, 0.75),
        "patch_bias": noise(seeds[7], (D,), 0.5, 3.0, (), jnp.float32),
        "shift_mod": noise(seeds[8], (D,), 1.0, 4.0, (), jnp.float32),
        "scale_mod": noise(seeds[9], (D,), 0.5, 2.0, (), jnp.float32),
        "query_weight": noise(seeds[10], (D, D), D ** -0.5, 0.078125, ((1, 8),)),
        "query_bias": noise(seeds[11], (D,), 1.0, 4.0, ((0, 8),), jnp.float32),
        "query_gain": jnp.clip(0.5 + 1.0 * jax.random.uniform(seeds[12], (D,), jnp.float32) ** level_of(seeds[12], (D,), ((0, 8),), -0.2, 0.2), 0.5, 1.5),
        "key_weight": noise(seeds[13], (D, D), D ** -0.5, 0.078125, ((1, 8),)),
        "key_bias": noise(seeds[14], (D,), 1.0, 4.0, ((0, 8),), jnp.float32),
        "key_gain": jnp.clip(0.5 + 1.0 * jax.random.uniform(seeds[15], (D,), jnp.float32) ** level_of(seeds[15], (D,), ((0, 8),), -0.2, 0.2), 0.5, 1.5),
        "packing": jax.random.permutation(seeds[16], BLOCKS).astype(jnp.int32),
    }


epsilon = 1e-06

def normed_act(features, block_gain):
    values = features.astype(jnp.float32)
    square_mean = lax.optimization_barrier(jnp.mean(values * values, axis=-1, keepdims=True))
    return jax.nn.silu(values * lax.rsqrt(square_mean + epsilon) * block_gain).astype(jnp.bfloat16)

def causal_conv(padded, conv_weight, frames, rows_count, cols_count, channels):
    total = jnp.zeros((frames * rows_count * cols_count, channels), jnp.float32)
    for depth_at in range(3):
        for row_at in range(3):
            slab_part = padded[depth_at:depth_at + frames, row_at:row_at + rows_count]
            joined = jnp.concatenate([slab_part[:, :, 0:cols_count], slab_part[:, :, 1:cols_count + 1], slab_part[:, :, 2:cols_count + 2]], axis=-1)
            kernel = conv_weight[depth_at, row_at].reshape(3 * channels, channels)
            total = total + jnp.dot(joined.reshape(-1, 3 * channels), kernel, preferred_element_type=jnp.float32)
    return total.reshape(frames, rows_count, cols_count, channels)

def project_norm(modulated, weight, bias, gain):
    values = jnp.dot(modulated, weight, preferred_element_type=jnp.float32) + bias
    square_mean = lax.optimization_barrier(jnp.mean(values * values, axis=-1, keepdims=True))
    return (values * lax.rsqrt(square_mean + epsilon) * gain).astype(jnp.bfloat16)

def reference(features, block_gain, conv_weight, conv_bias, latent_weight, latent_bias, patch_weight, patch_bias, shift_mod, scale_mod, query_weight, query_bias, query_gain, key_weight, key_bias, key_gain, packing):
    act = normed_act(features, block_gain)
    padded = jnp.pad(act, ((2, 0), (1, 1), (1, 1), (0, 0)))
    conv = causal_conv(padded, conv_weight, FRAMES, ROWS_ALL, COLS, C)
    block_out = (features.astype(jnp.float32) + conv + conv_bias).astype(jnp.bfloat16)
    latent = (jnp.dot(block_out.reshape(-1, C), latent_weight, preferred_element_type=jnp.float32) + latent_bias).astype(jnp.bfloat16)
    latent = latent.reshape(N_TM, FR_DEV, N_ROWS, ROW_DEV // 2, 2, COLS // 2, 2, LAT)
    blocks = jnp.transpose(latent, (0, 2, 7, 4, 6, 1, 3, 5)).reshape(BLOCKS, 4 * LAT, TOK_DEV)
    chosen = jnp.take(blocks, packing.astype(jnp.int32), axis=0)
    packed = jnp.transpose(chosen, (0, 2, 1)).reshape(TOKENS, 4 * LAT)
    embedded = jnp.dot(packed, patch_weight, preferred_element_type=jnp.float32) + patch_bias
    center = lax.optimization_barrier(jnp.mean(embedded, axis=-1, keepdims=True))
    spread = lax.optimization_barrier(jnp.mean((embedded - center) ** 2, axis=-1, keepdims=True))
    modulated = ((embedded - center) * lax.rsqrt(spread + epsilon) * (1.0 + scale_mod) + shift_mod).astype(jnp.bfloat16)
    queries = project_norm(modulated, query_weight, query_bias, query_gain)
    keys = project_norm(modulated, key_weight, key_bias, key_gain)
    return (queries, keys)
```

```python
import jax
import jax.numpy as jnp
from jax import lax
from jax.experimental import pallas as pl
from jax.experimental.pallas import tpu as pltpu
from jax.sharding import PartitionSpec as P

epsilon = 1e-06
bf16 = jnp.bfloat16
f32 = jnp.float32
VMEM = pl.BlockSpec(memory_space=pltpu.VMEM)
SMEM = pl.BlockSpec(memory_space=pltpu.SMEM)
MIB = 1 << 20
EXT = 80


def mm(a, b, ca, cb):
    return lax.dot_general(a, b, (((ca,), (cb,)), ((), ())), preferred_element_type=f32)


def halves(x):
    high = x.astype(bf16)
    return high, (x - high.astype(f32)).astype(bf16)


def iota(shape, dim):
    return lax.broadcasted_iota(jnp.int32, shape, dim)


def partial_kernel(feat, gain, bias, lw, lb, cw_hbm, out, cw, wt, gt, sems):
    chunk = 3
    copies = [
        pltpu.make_async_copy(
            cw_hbm.at[pl.ds(i * chunk, chunk)], cw.at[pl.ds(i * chunk, chunk)], sems.at[i]
        )
        for i in range(27 // chunk)
    ]
    for c in copies:
        c.start()
    values = feat[...].astype(f32)
    mean = jnp.mean(values * values, axis=-1, keepdims=True)
    y = values * lax.rsqrt(mean + epsilon) * gain[...]
    act = (y / (1.0 + jnp.exp(-y))).astype(bf16)
    lwt_f = jnp.transpose(lw[...].astype(f32))
    lwt = lwt_f.astype(bf16)
    direct = mm(lwt, feat[...], 1, 1)
    const = jnp.sum(lwt_f * bias[...], axis=1, keepdims=True) + jnp.transpose(lb[...])
    for i, c in enumerate(copies):
        c.wait()
        for k in range(i * chunk, (i + 1) * chunk):
            high, low = halves(mm(lwt, cw[k], 1, 1))
            wt[pl.ds(k * 16, 16), :] = high
            wt[pl.ds(432 + k * 16, 16), :] = low
    gt[...] = mm(wt[...], act, 1, 1)
    lane = iota((16, 128), 1)
    for fo in range(4):
        for ro in range(4):
            by_e = []
            for e in range(3):
                total = None
                for f in range(2):
                    for r in range(2):
                        a, b = f + 2 - fo, r + 2 - ro
                        if not (0 <= a < 3 and 0 <= b < 3):
                            continue
                        k, q = (a * 3 + b) * 3 + e, f * 2 + r
                        part = (
                            gt[pl.ds(k * 16, 16), pl.ds(q * 128, 128)]
                            + gt[pl.ds(432 + k * 16, 16), pl.ds(q * 128, 128)]
                        )
                        total = part if total is None else total + part
                by_e.append(total)
            left = jnp.where(lane == 0, 0.0, pltpu.roll(by_e[0], 1, 1))
            right = jnp.where(lane == 127, 0.0, pltpu.roll(by_e[2], 127, 1))
            value = left + by_e[1] + right
            if fo < 2 and 1 <= ro < 3:
                q = fo * 2 + ro - 1
                value = value + direct[:, q * 128 : (q + 1) * 128] + const
            out[fo, ro] = value


def partial_latents(features, gain, bias, lw, lb, cw):
    return pl.pallas_call(
        partial_kernel,
        out_shape=jax.ShapeDtypeStruct((4, 4, 16, 128), f32),
        in_specs=[VMEM] * 5 + [pl.BlockSpec(memory_space=pl.ANY)],
        out_specs=VMEM,
        scratch_shapes=[
            pltpu.VMEM((27, 384, 384), bf16),
            pltpu.VMEM((864, 384), bf16),
            pltpu.VMEM((864, 512), f32),
            pltpu.SemaphoreType.DMA((9,)),
        ],
        compiler_params=pltpu.CompilerParams(vmem_limit_bytes=40 * MIB),
        name="partial_latents",
    )(features, gain, bias, lw, lb, cw)


def prepare_kernel(pw, pb, shift, scale, parts, gram):
    width = pw.shape[1]
    to, at = iota((64, 64), 0), iota((64, 64), 1)
    wanted = 4 * (to % 16) + 2 * ((to // 16) % 2) + to // 32
    order = jnp.where(at == wanted, 1.0, 0.0).astype(bf16)
    rows = mm(order, pw[...], 1, 0)
    rows = rows - jnp.mean(rows, axis=1, keepdims=True)
    const = pb[...] - jnp.mean(pb[...], axis=1, keepdims=True)
    tail = iota((16, width), 0)
    const_tail = jnp.where(tail == 0, const, 0.0)
    centered = jnp.concatenate([rows, const_tail], axis=0)
    high, low = halves(centered)
    both = mm(jnp.concatenate([high, low], axis=0), high, 1, 1)
    cross = both[EXT:, :]
    gram[...] = (both[:EXT, :] + cross + jnp.transpose(cross)) * (1.0 / width)
    scaled = centered * (1.0 + scale[...])
    last = jnp.where(iota((EXT, width), 0) == 65, shift[...], scaled)
    high, low = halves(last)
    parts[pl.ds(0, EXT), :] = high
    parts[pl.ds(EXT, EXT), :] = low


def prepared(pw, pb, shift, scale):
    return pl.pallas_call(
        prepare_kernel,
        out_shape=[
            jax.ShapeDtypeStruct((2 * EXT, pw.shape[1]), bf16),
            jax.ShapeDtypeStruct((EXT, EXT), f32),
        ],
        in_specs=[VMEM] * 4,
        out_specs=[VMEM] * 2,
        compiler_params=pltpu.CompilerParams(vmem_limit_bytes=40 * MIB),
        name="prepare_patch",
    )(pw, pb, shift, scale)


def project_kernel(parts, w, bias, gain, right, gram):
    both = mm(parts[...], w[...], 1, 0)
    rows = both[:EXT, :] + both[EXT:, :]
    rows = rows + jnp.where(iota(rows.shape, 0) == 65, bias[...], 0.0)
    high, low = halves(rows)
    pairs = mm(jnp.concatenate([high, low], axis=0), high, 1, 1)
    cross = pairs[EXT:, :]
    gram[...] = pairs[:EXT, :] + cross + jnp.transpose(cross)
    high, low = halves(rows * gain[...])
    right[pl.ds(0, EXT), :] = high
    right[pl.ds(EXT, EXT), :] = high
    right[pl.ds(2 * EXT, EXT), :] = low


def projected(parts, w, bias, gain, name):
    return pl.pallas_call(
        project_kernel,
        out_shape=[
            jax.ShapeDtypeStruct((3 * EXT, w.shape[1]), bf16),
            jax.ShapeDtypeStruct((EXT, EXT), f32),
        ],
        in_specs=[VMEM] * 4,
        out_specs=[VMEM] * 2,
        compiler_params=pltpu.CompilerParams(vmem_limit_bytes=40 * MIB),
        name=name,
    )(parts, w, bias, gain)


def pack_kernel(gq, gk, out):
    i, j = iota((EXT, EXT), 0), iota((EXT, EXT), 1)
    square = jnp.where(i >= j, gq[...], gk[...])
    diagonal = jnp.sum(jnp.where(i == j, gk[...], 0.0), axis=1, keepdims=True)
    out[:, :EXT] = square
    out[:, EXT:] = jnp.broadcast_to(diagonal, (EXT, 128 - EXT))


def packed_grams(gq, gk):
    return pl.pallas_call(
        pack_kernel,
        out_shape=jax.ShapeDtypeStruct((EXT, 128), f32),
        in_specs=[VMEM] * 2,
        out_specs=VMEM,
        name="pack_grams",
    )(gq, gk)


def block_kernel(own, above, below, out):
    row = lax.axis_index("rows")
    first = jnp.where(row == 0, 0.0, 1.0)
    final = jnp.where(row == lax.axis_size("rows") - 1, 0.0, 1.0)
    upper = [(own[f, 1] + above[f] * first).astype(bf16) for f in range(2)]
    lower = [(own[f, 2] + below[f] * final).astype(bf16) for f in range(2)]
    values = jnp.concatenate(
        [jnp.concatenate(upper, axis=1), jnp.concatenate(lower, axis=1)], axis=0
    )
    source, target = iota((256, 256), 0), iota((256, 256), 1)
    wanted = ((target // 64) % 2) * 128 + 2 * (target % 64) + target // 128
    pick = jnp.where(source == wanted, 1.0, 0.0).astype(bf16)
    spread = mm(values, pick, 1, 0).astype(bf16)
    out[pl.ds(0, 32), :] = spread[:, :128]
    out[pl.ds(32, 32), :] = spread[:, 128:]


def own_block(own, above, below):
    return pl.pallas_call(
        block_kernel,
        out_shape=jax.ShapeDtypeStruct((64, 128), bf16),
        in_specs=[VMEM] * 3,
        out_specs=VMEM,
        name="own_block",
    )(own, above, below)


def select_kernel(packing, b0, b1, b2, b3, keep, send):
    t, r = lax.axis_index("tm"), lax.axis_index("rows")
    blocks = (b0, b1, b2, b3)
    core = t % 2
    for out, half in ((keep, core), (send, 1 - core)):
        for i in range(4):
            ident = packing[r * 8 + half * 4 + i]
            frame, place = ident // 16, ident % 16
            dz = (r // 4) ^ (place // 4)
            dy = (r % 4) ^ (place % 4)
            out[i] = jnp.zeros((64, 128), bf16)
            for m in range(4):

                @pl.when((frame == t) & (dz == m))
                def _(out=out, i=i, m=m, dy=dy):
                    out[i] = blocks[m][dy]


def selected(packing, quads):
    return pl.pallas_call(
        select_kernel,
        out_shape=[jax.ShapeDtypeStruct((4, 64, 128), bf16)] * 2,
        in_specs=[SMEM] + [VMEM] * 4,
        out_specs=[VMEM] * 2,
        name="select_blocks",
    )(packing, *quads)


def token_kernel(core, mine, other, patch_gram, grams, rq, rk, q_out, k_out, left, ends):
    step = pl.program_id(0)
    width = 5120.0

    @pl.when(step == 0)
    def _():
        i, j = iota((EXT, EXT), 0), iota((EXT, EXT), 1)
        total = grams[...] * (1.0 / width)
        square = total[:, :EXT]
        diagonal = jnp.where(i == j, total[:, EXT : EXT + 1], 0.0)
        gq = jnp.where(i > j, 2.0 * square, 0.0) + jnp.where(i == j, square, 0.0)
        gk = jnp.where(i > j, 2.0 * jnp.transpose(square), 0.0) + diagonal
        for n, g in enumerate((patch_gram[...], gq, gk)):
            high, low = halves(g)
            left[pl.ds(n * EXT, EXT), pl.ds(0, EXT)] = high
            left[pl.ds(n * EXT, EXT), pl.ds(EXT, EXT)] = low
        corner = (i == 65) & (j == 65)
        ends[0] = jnp.sum(jnp.where(corner, gq, 0.0))
        ends[1] = jnp.sum(jnp.where(corner, gk, 0.0))

    x = jnp.where(step < 4, mine[step % 4], other[step % 4])
    tail = iota((EXT - 64, 128), 0)
    xf = jnp.concatenate([x.astype(f32), jnp.where(tail == 0, 1.0, 0.0)], axis=0)
    xe = xf.astype(bf16)
    t = mm(left[...], jnp.concatenate([xe, xe], axis=0), 1, 0)
    spread = jnp.sum(t[:EXT] * xf, axis=0, keepdims=True)
    scale = lax.rsqrt(spread + epsilon)
    for n, (right, out) in enumerate(((rq, q_out), (rk, k_out))):
        tn = t[(n + 1) * EXT : (n + 2) * EXT]
        squares = (
            scale * scale * jnp.sum(tn * xf, axis=0, keepdims=True)
            + scale * tn[65:66]
            + ends[n]
        )
        beta = lax.rsqrt(squares + epsilon)
        alpha = scale * beta
        y = xf * alpha + jnp.where(iota((EXT, 128), 0) == 65, beta, 0.0)
        high, low = halves(y)
        out[...] = mm(jnp.concatenate([high, low, high], axis=0), right[...], 0, 0).astype(bf16)


def tokens(core, mine, other, patch_gram, grams, rq, rk):
    def out_at(step, core_ref):
        c = core_ref[0]
        return (jnp.where(step < 4, c * 4 + step, (1 - c) * 4 + step - 4), 0)

    width = rq.shape[1]
    whole = lambda a: pl.BlockSpec(a.shape, lambda step, core_ref: (0,) * a.ndim)
    args = (mine, other, patch_gram, grams, rq, rk)
    return pl.pallas_call(
        token_kernel,
        grid_spec=pltpu.PrefetchScalarGridSpec(
            num_scalar_prefetch=1,
            grid=(8,),
            in_specs=[whole(a) for a in args],
            out_specs=[pl.BlockSpec((128, width), out_at)] * 2,
            scratch_shapes=[
                pltpu.VMEM((3 * EXT, 2 * EXT), bf16),
                pltpu.SMEM((2,), f32),
            ],
        ),
        out_shape=[jax.ShapeDtypeStruct((1024, width), bf16)] * 2,
        compiler_params=pltpu.CompilerParams(vmem_limit_bytes=40 * MIB),
        name="tokens",
    )(core, *args)


def swapped(x, axis, bits):
    return lax.ppermute(x, axis, [(i, i ^ bits) for i in range(lax.axis_size(axis))])


def moved(x, axis, by):
    size = lax.axis_size(axis)
    return lax.ppermute(x, axis, [(i, (i + by) % size) for i in range(size)])


def per_device(
    features,
    block_gain,
    conv_weight,
    conv_bias,
    latent_weight,
    latent_bias,
    patch_weight,
    patch_bias,
    shift_mod,
    scale_mod,
    query_weight,
    query_bias,
    query_gain,
    key_weight,
    key_bias,
    key_gain,
    packing,
):
    channels = features.shape[-1]
    row = lambda v: v.reshape(1, -1)
    partial = partial_latents(
        features.reshape(-1, channels),
        row(block_gain),
        row(conv_bias),
        latent_weight,
        row(latent_bias),
        conv_weight.reshape(27, channels, channels),
    )
    before = moved(partial[2:], "tm", 1)
    own = partial[:2] + jnp.where(lax.axis_index("tm") == 0, 0.0, before)
    above = moved(own[:, 3], "rows", 1)
    below = moved(own[:, 0], "rows", -1)

    parts, patch_gram = prepared(
        patch_weight, row(patch_bias), row(shift_mod), row(scale_mod)
    )
    rq, gq = projected(parts, query_weight, row(query_bias), row(query_gain), "project_query")
    rk, gk = projected(parts, key_weight, row(key_bias), row(key_gain), "project_key")
    grams = packed_grams(gq, gk)
    grams = grams + swapped(grams, "tm", 1)
    grams = grams + swapped(grams, "tm", 2) + swapped(grams, "tm", 4) + swapped(grams, "tm", 6)

    block = own_block(own, above, below)
    quad = jnp.stack([block] + [swapped(block, "rows", k) for k in (1, 2, 3)])
    quads = [quad] + [swapped(quad, "rows", 4 * k) for k in (1, 2, 3)]
    keep, send = selected(packing, quads)
    mine = keep + swapped(send, "tm", 1)
    mine = mine + swapped(mine, "tm", 2) + swapped(mine, "tm", 4) + swapped(mine, "tm", 6)
    other = swapped(mine, "tm", 1)
    core = (lax.axis_index("tm") % 2).astype(jnp.int32).reshape(1)
    return tokens(core, mine, other, patch_gram, grams, rq, rk)


def solution(mesh):
    in_specs = (
        P("tm", "rows", None, None),
        P(),
        P(),
        P(),
        P(),
        P(),
        P(),
        P(),
        P(),
        P(),
        P(None, "tm"),
        P("tm"),
        P("tm"),
        P(None, "tm"),
        P("tm"),
        P("tm"),
        P(),
    )
    out_specs = (P("rows", "tm"), P("rows", "tm"))
    return jax.shard_map(
        per_device, mesh=mesh, in_specs=in_specs, out_specs=out_specs, check_vma=False
    )
```

```python
import functools

import jax
import jax.numpy as jnp
from jax import lax
from jax.experimental import pallas as pl
from jax.experimental.pallas import tpu as pltpu
from jax.sharding import PartitionSpec as P

epsilon = 1e-06
bf16 = jnp.bfloat16
f32 = jnp.float32
VMEM = pl.BlockSpec(memory_space=pltpu.VMEM)
SMEM = pl.BlockSpec(memory_space=pltpu.SMEM)
HBM = pl.BlockSpec(memory_space=pltpu.HBM)
MIB = 1 << 20
EXT = 80


def mm(a, b, ca, cb):
    return lax.dot_general(a, b, (((ca,), (cb,)), ((), ())), preferred_element_type=f32)


def halves(x):
    high = x.astype(bf16)
    return high, (x - high.astype(f32)).astype(bf16)


def iota(shape, dim):
    return lax.broadcasted_iota(jnp.int32, shape, dim)


def call(kernel, name, out_shape, in_specs, limit, scratch=(), cost=None, **more):
    more.setdefault("out_specs", jax.tree.map(lambda _: VMEM, out_shape))
    return pl.pallas_call(
        kernel,
        out_shape=out_shape,
        in_specs=in_specs,
        scratch_shapes=list(scratch),
        compiler_params=pltpu.CompilerParams(vmem_limit_bytes=limit * MIB),
        cost_estimate=cost,
        name=name,
        **more,
    )


def array(shape, kind):
    return jax.ShapeDtypeStruct(shape, kind)


def partial_kernel(
    feat_hbm, gain_hbm, bias_hbm, lwt_hbm, lb_hbm, cw_hbm, out,
    feat, gain, bias, lwt_ref, lb, cw, wt, gt, sems,
):
    small = [
        pltpu.make_async_copy(a, b, sems.at[9 + i])
        for i, (a, b) in enumerate(
            (
                (feat_hbm, feat),
                (gain_hbm, gain),
                (bias_hbm, bias),
                (lwt_hbm, lwt_ref),
                (lb_hbm, lb),
            )
        )
    ]
    for c in small:
        c.start()
    chunk = 3
    copies = [
        pltpu.make_async_copy(
            cw_hbm.at[pl.ds(i * chunk, chunk)], cw.at[pl.ds(i * chunk, chunk)], sems.at[i]
        )
        for i in range(27 // chunk)
    ]
    for c in copies:
        c.start()
    for c in small:
        c.wait()
    values = feat[...].astype(f32)
    mean = jnp.mean(values * values, axis=-1, keepdims=True)
    y = values * lax.rsqrt(mean + epsilon) * gain[...].reshape(1, -1)
    act = (y / (1.0 + jnp.exp(-y))).astype(bf16)
    lwt = lwt_ref[...]
    direct = mm(lwt, feat[...], 1, 1)
    const = jnp.sum(lwt.astype(f32) * bias[...].reshape(1, -1), axis=1, keepdims=True)
    const = const + jnp.transpose(lb[...].reshape(1, -1))
    for i, c in enumerate(copies):
        c.wait()
        for k in range(i * chunk, (i + 1) * chunk):
            high, low = halves(mm(lwt, cw[k], 1, 1))
            wt[pl.ds(k * 16, 16), :] = high
            wt[pl.ds(432 + k * 16, 16), :] = low
    gt[...] = mm(wt[...], act, 1, 1)
    lane = iota((16, 128), 1)
    for fo in range(4):
        for ro in range(4):
            by_e = []
            for e in range(3):
                total = None
                for f in range(2):
                    for r in range(2):
                        a, b = f + 2 - fo, r + 2 - ro
                        if not (0 <= a < 3 and 0 <= b < 3):
                            continue
                        k, q = (a * 3 + b) * 3 + e, f * 2 + r
                        part = (
                            gt[pl.ds(k * 16, 16), pl.ds(q * 128, 128)]
                            + gt[pl.ds(432 + k * 16, 16), pl.ds(q * 128, 128)]
                        )
                        total = part if total is None else total + part
                by_e.append(total)
            left = jnp.where(lane == 0, 0.0, pltpu.roll(by_e[0], 1, 1))
            right = jnp.where(lane == 127, 0.0, pltpu.roll(by_e[2], 127, 1))
            value = left + by_e[1] + right
            if fo < 2 and 1 <= ro < 3:
                q = fo * 2 + ro - 1
                value = value + direct[:, q * 128 : (q + 1) * 128] + const
            out[fo, ro] = value


def partial_latents(*args):
    return call(
        partial_kernel,
        "partial_latents",
        array((4, 4, 16, 128), f32),
        [HBM] * 6,
        20,
        scratch=[
            pltpu.VMEM((512, 384), bf16),
            pltpu.VMEM((384,), f32),
            pltpu.VMEM((384,), f32),
            pltpu.VMEM((16, 384), bf16),
            pltpu.VMEM((16,), f32),
            pltpu.VMEM((27, 384, 384), bf16),
            pltpu.VMEM((864, 384), bf16),
            pltpu.VMEM((864, 512), f32),
            pltpu.SemaphoreType.DMA((14,)),
        ],
    )(*args)


def weights_kernel(
    pw, pb, shift, scale, wq_hbm, wk_hbm, bq, bk, gq, gk,
    rq, rk, patch_gram, grams, wq, wk, parts, sems,
):
    width = pw.shape[1]
    chunk = width // 4
    copies = []
    for n, (a, b) in enumerate(((wq_hbm, wq), (wk_hbm, wk))):
        copies.append([])
        for i in range(4):
            at = pl.ds(i * chunk, chunk)
            c = pltpu.make_async_copy(a.at[at], b.at[at], sems.at[n * 4 + i])
            c.start()
            copies[n].append(c)
    to, at = iota((64, 64), 0), iota((64, 64), 1)
    wanted = 4 * (to % 16) + 2 * ((to // 16) % 2) + to // 32
    order = jnp.where(at == wanted, 1.0, 0.0).astype(bf16)
    rows = mm(order, pw[...], 1, 0)
    rows = rows - jnp.mean(rows, axis=1, keepdims=True)
    const = pb[...] - jnp.mean(pb[...], axis=1, keepdims=True)
    const_tail = jnp.where(iota((16, width), 0) == 0, const, 0.0)
    centered = jnp.concatenate([rows, const_tail], axis=0)
    high, low = halves(centered)
    both = mm(jnp.concatenate([high, low], axis=0), high, 1, 1)
    cross = both[EXT:, :]
    patch_gram[...] = (both[:EXT, :] + cross + jnp.transpose(cross)) * (1.0 / width)
    scaled = centered * (1.0 + scale[...])
    high, low = halves(jnp.where(iota((EXT, width), 0) == 65, shift[...], scaled))
    parts[pl.ds(0, EXT), :] = high
    parts[pl.ds(EXT, EXT), :] = low
    found = []
    for n, (w, bias, gain, right) in enumerate(((wq, bq, gq, rq), (wk, bk, gk, rk))):
        both = None
        for i, c in enumerate(copies[n]):
            c.wait()
            at = pl.ds(i * chunk, chunk)
            part = mm(parts[:, at], w[at, :], 1, 0)
            both = part if both is None else both + part
        rows = both[:EXT, :] + both[EXT:, :]
        rows = rows + jnp.where(iota(rows.shape, 0) == 65, bias[...], 0.0)
        high, low = halves(rows)
        pairs = mm(jnp.concatenate([high, low], axis=0), high, 1, 1)
        cross = pairs[EXT:, :]
        found.append(pairs[:EXT, :] + cross + jnp.transpose(cross))
        high, low = halves(rows * gain[...])
        right[pl.ds(0, EXT), :] = high
        right[pl.ds(EXT, EXT), :] = high
        right[pl.ds(2 * EXT, EXT), :] = low
    i, j = iota((EXT, EXT), 0), iota((EXT, EXT), 1)
    diagonal = jnp.sum(jnp.where(i == j, found[1], 0.0), axis=1, keepdims=True)
    grams[:, :EXT] = jnp.where(i >= j, found[0], found[1])
    grams[:, EXT:] = jnp.broadcast_to(diagonal, (EXT, 128 - EXT))


def weights_only(pw, pb, shift, scale, wq, wk, bq, bk, gq, gk):
    width, part = wq.shape
    return call(
        weights_kernel,
        "weights_only",
        [
            array((3 * EXT, part), bf16),
            array((3 * EXT, part), bf16),
            array((EXT, EXT), f32),
            array((EXT, 128), f32),
        ],
        [VMEM] * 4 + [HBM] * 2 + [VMEM] * 4,
        36,
        scratch=[
            pltpu.VMEM((width, part), bf16),
            pltpu.VMEM((width, part), bf16),
            pltpu.VMEM((2 * EXT, width), bf16),
            pltpu.SemaphoreType.DMA((8,)),
        ],
        cost=pl.CostEstimate(
            flops=4 * 2 * EXT * width * part * 4, bytes_accessed=2 * width * part * 2, transcendentals=0
        ),
    )(pw, pb, shift, scale, wq, wk, bq, bk, gq, gk)


def block_kernel(own, above, below, out):
    row = lax.axis_index("rows")
    first = jnp.where(row == 0, 0.0, 1.0)
    final = jnp.where(row == lax.axis_size("rows") - 1, 0.0, 1.0)
    upper = [(own[f, 1] + above[f] * first).astype(bf16) for f in range(2)]
    lower = [(own[f, 2] + below[f] * final).astype(bf16) for f in range(2)]
    values = jnp.concatenate(
        [jnp.concatenate(upper, axis=1), jnp.concatenate(lower, axis=1)], axis=0
    )
    source, target = iota((256, 256), 0), iota((256, 256), 1)
    wanted = ((target // 64) % 2) * 128 + 2 * (target % 64) + target // 128
    pick = jnp.where(source == wanted, 1.0, 0.0).astype(bf16)
    spread = mm(values, pick, 1, 0).astype(bf16)
    block = jnp.concatenate([spread[:, :128], spread[:, 128:]], axis=0)
    for i in range(out.shape[0]):
        out[i] = block


def own_block(own, above, below):
    return call(
        block_kernel, "own_block", array((lax.axis_size("rows"), 64, 128), bf16), [VMEM] * 3, 4
    )(own, above, below)


def select_kernel(packing, blocks, keep, send):
    t, r = lax.axis_index("tm"), lax.axis_index("rows")
    core = t % 2
    for out, half in ((keep, core), (send, 1 - core)):
        for i in range(4):
            ident = packing[r * 8 + half * 4 + i]
            here = jnp.where(ident // 16 == t, 1.0, 0.0).astype(bf16)
            out[i] = blocks[ident % 16] * here


def selected(packing, blocks):
    return call(
        select_kernel, "select_blocks", [array((4, 64, 128), bf16)] * 2, [SMEM, VMEM], 4
    )(packing, blocks)


def forms_kernel(patch_gram, grams, left):
    i, j = iota((EXT, EXT), 0), iota((EXT, EXT), 1)
    total = grams[...] * (1.0 / 5120.0)
    square = total[:, :EXT]
    gq = jnp.where(i > j, 2.0 * square, 0.0) + jnp.where(i == j, square, 0.0)
    gk = jnp.where(i > j, 2.0 * jnp.transpose(square), 0.0)
    gk = gk + jnp.where(i == j, total[:, EXT : EXT + 1], 0.0)
    left[pl.ds(0, EXT), :] = jnp.concatenate(halves(patch_gram[...]), axis=1)
    for n, g in enumerate((gq, gk)):
        end = jnp.sum(jnp.where((i == 65) & (j == 65), g, 0.0), keepdims=True)
        g = jnp.where((i == 66) & (j == 64), end, g)
        left[pl.ds((n + 1) * EXT, EXT), :] = jnp.concatenate(halves(g), axis=1)


def quadratic_forms(patch_gram, grams):
    return call(
        forms_kernel, "quadratic_forms", array((3 * EXT, 2 * EXT), bf16), [VMEM] * 2, 4
    )(patch_gram, grams)


def token_kernel(other_half, x_ref, left, rq, rk, *refs):
    q_out, k_out, q_buf, k_buf, sems = refs[-5:]
    core = lax.axis_index("tm") % 2
    place = (1 - core if other_half else core) * 512
    copies = []
    for part in range(2):
        x = jnp.concatenate([x_ref[2 * part], x_ref[2 * part + 1]], axis=1)
        tail = iota((EXT - 64, 256), 0)
        xf = jnp.concatenate([x.astype(f32), jnp.where(tail == 0, 1.0, 0.0)], axis=0)
        xe = xf.astype(bf16)
        t = mm(left[...], jnp.concatenate([xe, xe], axis=0), 1, 0)
        spread = jnp.sum(t[:EXT] * xf, axis=0, keepdims=True)
        scale = lax.rsqrt(spread + epsilon)
        for n, (right, buf, out) in enumerate(((rq, q_buf, q_out), (rk, k_buf, k_out))):
            tn = t[(n + 1) * EXT : (n + 2) * EXT]
            squares = (
                scale * scale * jnp.sum(tn * xf, axis=0, keepdims=True)
                + scale * tn[65:66]
                + tn[66:67]
            )
            beta = lax.rsqrt(squares + epsilon)
            alpha = scale * beta
            y = xf * alpha + jnp.where(iota((EXT, 256), 0) == 65, beta, 0.0)
            high, low = halves(y)
            lhs = jnp.concatenate([high, low, high], axis=0)
            buf[part] = mm(lhs, right[...], 0, 0).astype(bf16)
            c = pltpu.make_async_copy(
                buf.at[part], out.at[pl.ds(pl.multiple_of(place + part * 256, 256), 256)], sems.at[part * 2 + n]
            )
            c.start()
            copies.append(c)
    for c in copies:
        c.wait()


def tokens(x, left, rq, rk, before=None):
    width = rq.shape[1]
    given = () if before is None else tuple(before)
    return call(
        functools.partial(token_kernel, before is not None),
        "tokens_other" if given else "tokens_mine",
        [array((1024, width), bf16)] * 2,
        [VMEM] * 4 + [HBM] * len(given),
        12,
        scratch=[
            pltpu.VMEM((2, 256, width), bf16),
            pltpu.VMEM((2, 256, width), bf16),
            pltpu.SemaphoreType.DMA((4,)),
        ],
        out_specs=[HBM, HBM],
        input_output_aliases={4: 0, 5: 1} if given else {},
    )(x, left, rq, rk, *given)


def in_hbm(x):
    return pltpu.with_memory_space_constraint(x, pltpu.HBM)


def swapped(x, axis, bits):
    return lax.ppermute(x, axis, [(i, i ^ bits) for i in range(lax.axis_size(axis))])


def moved(x, axis, by):
    size = lax.axis_size(axis)
    return lax.ppermute(x, axis, [(i, (i + by) % size) for i in range(size)])


def per_device(
    features,
    block_gain,
    conv_weight,
    conv_bias,
    latent_weight,
    latent_bias,
    patch_weight,
    patch_bias,
    shift_mod,
    scale_mod,
    query_weight,
    query_bias,
    query_gain,
    key_weight,
    key_bias,
    key_gain,
    packing,
):
    channels = features.shape[-1]
    row = lambda v: v.reshape(1, -1)
    partial = partial_latents(
        *map(
            in_hbm,
            (
                features.reshape(-1, channels),
                block_gain,
                conv_bias,
                latent_weight.T,
                latent_bias,
                conv_weight.reshape(27, channels, channels),
            ),
        )
    )
    before = moved(partial[2:], "tm", 1)
    own = partial[:2] + jnp.where(lax.axis_index("tm") == 0, 0.0, before)
    above = moved(own[:, 3], "rows", 1)
    below = moved(own[:, 0], "rows", -1)
    copies = own_block(own, above, below)
    copies, patch_weight = lax.optimization_barrier((copies, patch_weight))
    plane = lax.all_to_all(copies, "rows", 0, 0, tiled=True)

    rq, rk, patch_gram, grams = weights_only(
        patch_weight,
        row(patch_bias),
        row(shift_mod),
        row(scale_mod),
        in_hbm(query_weight),
        in_hbm(key_weight),
        row(query_bias),
        row(key_bias),
        row(query_gain),
        row(key_gain),
    )
    plane, grams = lax.optimization_barrier((plane, grams))
    grams = grams + swapped(grams, "tm", 1)
    grams = grams + swapped(grams, "tm", 2) + swapped(grams, "tm", 4) + swapped(grams, "tm", 6)
    left = quadratic_forms(patch_gram, grams)

    keep, send = selected(packing, plane)
    mine = keep + swapped(send, "tm", 1)
    mine = mine + swapped(mine, "tm", 2) + swapped(mine, "tm", 4) + swapped(mine, "tm", 6)
    other = swapped(mine, "tm", 1)
    return tokens(other, left, rq, rk, tokens(mine, left, rq, rk))


def solution(mesh):
    in_specs = (
        P("tm", "rows", None, None),
        P(),
        P(),
        P(),
        P(),
        P(),
        P(),
        P(),
        P(),
        P(),
        P(None, "tm"),
        P("tm"),
        P("tm"),
        P(None, "tm"),
        P("tm"),
        P("tm"),
        P(),
    )
    out_specs = (P("rows", "tm"), P("rows", "tm"))
    return jax.shard_map(
        per_device, mesh=mesh, in_specs=in_specs, out_specs=out_specs, check_vma=False
    )
```

```python
import functools

import jax
import jax.numpy as jnp
from jax import lax
from jax.experimental import pallas as pl
from jax.experimental.pallas import tpu as pltpu
from jax.sharding import PartitionSpec as P

epsilon = 1e-06
bf16 = jnp.bfloat16
f32 = jnp.float32
VMEM = pl.BlockSpec(memory_space=pltpu.VMEM)
SMEM = pl.BlockSpec(memory_space=pltpu.SMEM)
HBM = pl.BlockSpec(memory_space=pltpu.HBM)
MIB = 1 << 20
EXT = 80


def mm(a, b, ca, cb):
    return lax.dot_general(a, b, (((ca,), (cb,)), ((), ())), preferred_element_type=f32)


def halves(x):
    high = x.astype(bf16)
    return high, (x - high.astype(f32)).astype(bf16)


def iota(shape, dim):
    return lax.broadcasted_iota(jnp.int32, shape, dim)


def call(kernel, name, out_shape, in_specs, limit, scratch=(), cost=None, **more):
    more.setdefault("out_specs", jax.tree.map(lambda _: VMEM, out_shape))
    return pl.pallas_call(
        kernel,
        out_shape=out_shape,
        in_specs=in_specs,
        scratch_shapes=list(scratch),
        compiler_params=pltpu.CompilerParams(vmem_limit_bytes=limit * MIB),
        cost_estimate=cost,
        name=name,
        **more,
    )


def array(shape, kind):
    return jax.ShapeDtypeStruct(shape, kind)


def folded(lwt, cw, wt, gt, act, copies, at, taps):
    chunk = taps // len(copies)
    for i, c in enumerate(copies):
        c.wait()
        for k in range(i * chunk, (i + 1) * chunk):
            high, low = halves(mm(lwt, cw[at + k], 1, 1))
            wt[pl.ds(k * 16, 16), :] = high
            wt[pl.ds(144 + k * 16, 16), :] = low
    gt[...] = mm(wt[...], act, 1, 1)


def shifted_sum(by_e):
    lane = iota((16, 128), 1)
    left = jnp.where(lane == 0, 0.0, pltpu.roll(by_e[0], 1, 1))
    right = jnp.where(lane == 127, 0.0, pltpu.roll(by_e[2], 127, 1))
    return left + by_e[1] + right


def contributions(gts, fo, ro):
    by_e = []
    for e in range(3):
        total = None
        for f in range(2):
            for r in range(2):
                a, b = f + 2 - fo, r + 2 - ro
                if a not in gts or not 0 <= b < 3:
                    continue
                k, q = b * 3 + e, f * 2 + r
                part = (
                    gts[a][pl.ds(k * 16, 16), pl.ds(q * 128, 128)]
                    + gts[a][pl.ds(144 + k * 16, 16), pl.ds(q * 128, 128)]
                )
                total = part if total is None else total + part
        by_e.append(total)
    return shifted_sum(by_e)


def chunked(source, target, sems, start, count, size, first_sem):
    found = []
    for i in range(count):
        c = pltpu.make_async_copy(
            source.at[pl.ds(start + i * size, size)],
            target.at[pl.ds(i * size, size)],
            sems.at[first_sem + i],
        )
        c.start()
        found.append(c)
    return found


def early_kernel(
    feat_hbm, gain_hbm, bias_hbm, lwt_hbm, lb_hbm, cw_hbm, ahead, own, act_out,
    feat, gain, bias, lwt_ref, lb, cw, wt, gt0, gt1, sems,
):
    small = [
        pltpu.make_async_copy(a, b, sems.at[6 + i])
        for i, (a, b) in enumerate(
            (
                (feat_hbm, feat),
                (gain_hbm, gain),
                (bias_hbm, bias),
                (lwt_hbm, lwt_ref),
                (lb_hbm, lb),
            )
        )
    ]
    for c in small:
        c.start()
    copies = chunked(cw_hbm, cw, sems, 0, 6, 3, 0)
    for c in small:
        c.wait()
    values = feat[...].astype(f32)
    mean = jnp.mean(values * values, axis=-1, keepdims=True)
    y = values * lax.rsqrt(mean + epsilon) * gain[...].reshape(1, -1)
    act = (y / (1.0 + jnp.exp(-y))).astype(bf16)
    act_out[...] = act
    lwt = lwt_ref[...]
    direct = mm(lwt, feat[...], 1, 1)
    const = jnp.sum(lwt.astype(f32) * bias[...].reshape(1, -1), axis=1, keepdims=True)
    const = const + jnp.transpose(lb[...].reshape(1, -1))
    folded(lwt, cw, wt, gt0, act, copies[:3], 0, 9)
    folded(lwt, cw, wt, gt1, act, copies[3:], 9, 9)
    for ro in range(4):
        for fo in (2, 3):
            ahead[fo - 2, ro] = contributions({0: gt0, 1: gt1}, fo, ro)
        own[0, ro] = jnp.zeros((16, 128), f32)
        own[1, ro] = contributions({1: gt1}, 1, ro)
        if 1 <= ro < 3:
            for fo in range(2):
                q = fo * 2 + ro - 1
                own[fo, ro] += direct[:, q * 128 : (q + 1) * 128] + const


def early_latents(*args):
    return call(
        early_kernel,
        "early_latents",
        [array((2, 4, 16, 128), f32), array((2, 4, 16, 128), f32), array((512, 384), bf16)],
        [HBM] * 6,
        20,
        scratch=[
            pltpu.VMEM((512, 384), bf16),
            pltpu.VMEM((384,), f32),
            pltpu.VMEM((384,), f32),
            pltpu.VMEM((16, 384), bf16),
            pltpu.VMEM((16,), f32),
            pltpu.VMEM((18, 384, 384), bf16),
            pltpu.VMEM((288, 384), bf16),
            pltpu.VMEM((288, 512), f32),
            pltpu.VMEM((288, 512), f32),
            pltpu.SemaphoreType.DMA((11,)),
        ],
    )(*args)


def late_kernel(own, act, lwt_hbm, cw_hbm, out, lwt, cw, wt, gt, sems):
    small = pltpu.make_async_copy(lwt_hbm, lwt, sems.at[3])
    small.start()
    copies = chunked(cw_hbm, cw, sems, 18, 3, 3, 0)
    small.wait()
    folded(lwt[...], cw, wt, gt, act[...], copies, 0, 9)
    for fo in range(2):
        for ro in range(4):
            out[fo, ro] = own[fo, ro] + contributions({2: gt}, fo, ro)


def late_latents(*args):
    return call(
        late_kernel,
        "late_latents",
        array((2, 4, 16, 128), f32),
        [VMEM] * 2 + [HBM] * 2,
        10,
        scratch=[
            pltpu.VMEM((16, 384), bf16),
            pltpu.VMEM((9, 384, 384), bf16),
            pltpu.VMEM((288, 384), bf16),
            pltpu.VMEM((288, 512), f32),
            pltpu.SemaphoreType.DMA((4,)),
        ],
        cost=pl.CostEstimate(flops=3 * 10**9, bytes_accessed=5 * 10**6, transcendentals=0),
    )(*args)


def weights_kernel(
    pw, pb, shift, scale, wq_hbm, wk_hbm, bq, bk, gq, gk,
    rq, rk, patch_gram, grams, wq, wk, parts, sems,
):
    width = pw.shape[1]
    chunk = width // 4
    copies = []
    for n, (a, b) in enumerate(((wq_hbm, wq), (wk_hbm, wk))):
        copies.append([])
        for i in range(4):
            at = pl.ds(i * chunk, chunk)
            c = pltpu.make_async_copy(a.at[at], b.at[at], sems.at[n * 4 + i])
            c.start()
            copies[n].append(c)
    to, at = iota((64, 64), 0), iota((64, 64), 1)
    wanted = 4 * (to % 16) + 2 * ((to // 16) % 2) + to // 32
    order = jnp.where(at == wanted, 1.0, 0.0).astype(bf16)
    rows = mm(order, pw[...], 1, 0)
    rows = rows - jnp.mean(rows, axis=1, keepdims=True)
    const = pb[...] - jnp.mean(pb[...], axis=1, keepdims=True)
    const_tail = jnp.where(iota((16, width), 0) == 0, const, 0.0)
    centered = jnp.concatenate([rows, const_tail], axis=0)
    high, low = halves(centered)
    both = mm(jnp.concatenate([high, low], axis=0), high, 1, 1)
    cross = both[EXT:, :]
    patch_gram[...] = (both[:EXT, :] + cross + jnp.transpose(cross)) * (1.0 / width)
    scaled = centered * (1.0 + scale[...])
    high, low = halves(jnp.where(iota((EXT, width), 0) == 65, shift[...], scaled))
    parts[pl.ds(0, EXT), :] = high
    parts[pl.ds(EXT, EXT), :] = low
    found = []
    for n, (w, bias, gain, right) in enumerate(((wq, bq, gq, rq), (wk, bk, gk, rk))):
        both = None
        for i, c in enumerate(copies[n]):
            c.wait()
            at = pl.ds(i * chunk, chunk)
            part = mm(parts[:, at], w[at, :], 1, 0)
            both = part if both is None else both + part
        rows = both[:EXT, :] + both[EXT:, :]
        rows = rows + jnp.where(iota(rows.shape, 0) == 65, bias[...], 0.0)
        high, low = halves(rows)
        pairs = mm(jnp.concatenate([high, low], axis=0), high, 1, 1)
        cross = pairs[EXT:, :]
        found.append(pairs[:EXT, :] + cross + jnp.transpose(cross))
        high, low = halves(rows * gain[...])
        right[pl.ds(0, EXT), :] = high
        right[pl.ds(EXT, EXT), :] = high
        right[pl.ds(2 * EXT, EXT), :] = low
    i, j = iota((EXT, EXT), 0), iota((EXT, EXT), 1)
    diagonal = jnp.sum(jnp.where(i == j, found[1], 0.0), axis=1, keepdims=True)
    grams[:, :EXT] = jnp.where(i >= j, found[0], found[1])
    grams[:, EXT:] = jnp.broadcast_to(diagonal, (EXT, 128 - EXT))


def weights_only(pw, pb, shift, scale, wq, wk, bq, bk, gq, gk):
    width, part = wq.shape
    return call(
        weights_kernel,
        "weights_only",
        [
            array((3 * EXT, part), bf16),
            array((3 * EXT, part), bf16),
            array((EXT, EXT), f32),
            array((EXT, 128), f32),
        ],
        [VMEM] * 4 + [HBM] * 2 + [VMEM] * 4,
        36,
        scratch=[
            pltpu.VMEM((width, part), bf16),
            pltpu.VMEM((width, part), bf16),
            pltpu.VMEM((2 * EXT, width), bf16),
            pltpu.SemaphoreType.DMA((8,)),
        ],
        cost=pl.CostEstimate(
            flops=4 * 2 * EXT * width * part * 4, bytes_accessed=2 * width * part * 2, transcendentals=0
        ),
    )(pw, pb, shift, scale, wq, wk, bq, bk, gq, gk)


def block_kernel(own, before, out):
    first = jnp.where(lax.axis_index("tm") == 0, 0.0, 1.0)
    rows = []
    for ro in (1, 2, 3, 0):
        frames = [own[f, ro] + before[f, ro] * first for f in range(2)]
        rows.append(jnp.concatenate(frames, axis=1).astype(bf16))
    source, target = iota((256, 256), 0), iota((256, 256), 1)
    wanted = ((target // 64) % 2) * 128 + 2 * (target % 64) + target // 128
    pick = jnp.where(source == wanted, 1.0, 0.0).astype(bf16)
    spread = mm(jnp.concatenate(rows, axis=0), pick, 1, 0).astype(bf16)
    block = jnp.concatenate(
        [spread[:32, :128], spread[:32, 128:], spread[32:, :128], spread[32:, 128:]], axis=0
    )
    for i in range(out.shape[0]):
        out[i] = block


def own_block(own, before):
    return call(
        block_kernel, "own_block", array((lax.axis_size("rows"), 128, 128), bf16), [VMEM] * 2, 4
    )(own, before)


def select_kernel(packing, blocks, keep, send):
    t, r = lax.axis_index("tm"), lax.axis_index("rows")
    last = blocks.shape[0] - 1
    core = t % 2
    upper = (iota((64, 128), 0) // 16) % 2 == 0
    for out, half in ((keep, core), (send, 1 - core)):
        for i in range(4):
            ident = packing[r * 8 + half * 4 + i]
            place = ident % 16
            here = jnp.where(ident // 16 == t, 1.0, 0.0)
            first = jnp.where(place == 0, 0.0, here)
            final = jnp.where(place == last, 0.0, here)
            own = blocks[place, pl.ds(0, 64)].astype(f32)
            above = blocks[jnp.maximum(place - 1, 0), pl.ds(64, 64)].astype(f32)
            below = blocks[jnp.minimum(place + 1, last), pl.ds(64, 64)].astype(f32)
            value = own * here + jnp.where(upper, above * first, below * final)
            out[i] = value.astype(bf16)


def selected(packing, blocks):
    return call(
        select_kernel, "select_blocks", [array((4, 64, 128), bf16)] * 2, [SMEM, VMEM], 4
    )(packing, blocks)


def forms_kernel(patch_gram, grams, left):
    i, j = iota((EXT, EXT), 0), iota((EXT, EXT), 1)
    total = grams[...] * (1.0 / 5120.0)
    square = total[:, :EXT]
    gq = jnp.where(i > j, 2.0 * square, 0.0) + jnp.where(i == j, square, 0.0)
    gk = jnp.where(i > j, 2.0 * jnp.transpose(square), 0.0)
    gk = gk + jnp.where(i == j, total[:, EXT : EXT + 1], 0.0)
    left[pl.ds(0, EXT), :] = jnp.concatenate(halves(patch_gram[...]), axis=1)
    for n, g in enumerate((gq, gk)):
        end = jnp.sum(jnp.where((i == 65) & (j == 65), g, 0.0), keepdims=True)
        g = jnp.where((i == 66) & (j == 64), end, g)
        left[pl.ds((n + 1) * EXT, EXT), :] = jnp.concatenate(halves(g), axis=1)


def quadratic_forms(patch_gram, grams):
    return call(
        forms_kernel, "quadratic_forms", array((3 * EXT, 2 * EXT), bf16), [VMEM] * 2, 4
    )(patch_gram, grams)


def token_kernel(other_half, x_ref, left, rq, rk, *refs):
    q_out, k_out, q_buf, k_buf, sems = refs[-5:]
    core = lax.axis_index("tm") % 2
    place = (1 - core if other_half else core) * 512
    copies = []
    for part in range(2):
        x = jnp.concatenate([x_ref[2 * part], x_ref[2 * part + 1]], axis=1)
        tail = iota((EXT - 64, 256), 0)
        xf = jnp.concatenate([x.astype(f32), jnp.where(tail == 0, 1.0, 0.0)], axis=0)
        xe = xf.astype(bf16)
        t = mm(left[...], jnp.concatenate([xe, xe], axis=0), 1, 0)
        spread = jnp.sum(t[:EXT] * xf, axis=0, keepdims=True)
        scale = lax.rsqrt(spread + epsilon)
        for n, (right, buf, out) in enumerate(((rq, q_buf, q_out), (rk, k_buf, k_out))):
            tn = t[(n + 1) * EXT : (n + 2) * EXT]
            squares = (
                scale * scale * jnp.sum(tn * xf, axis=0, keepdims=True)
                + scale * tn[65:66]
                + tn[66:67]
            )
            beta = lax.rsqrt(squares + epsilon)
            alpha = scale * beta
            y = xf * alpha + jnp.where(iota((EXT, 256), 0) == 65, beta, 0.0)
            high, low = halves(y)
            lhs = jnp.concatenate([high, low, high], axis=0)
            buf[part] = mm(lhs, right[...], 0, 0).astype(bf16)
            c = pltpu.make_async_copy(
                buf.at[part], out.at[pl.ds(pl.multiple_of(place + part * 256, 256), 256)], sems.at[part * 2 + n]
            )
            c.start()
            copies.append(c)
    for c in copies:
        c.wait()


def tokens(x, left, rq, rk, before=None):
    width = rq.shape[1]
    given = () if before is None else tuple(before)
    return call(
        functools.partial(token_kernel, before is not None),
        "tokens_other" if given else "tokens_mine",
        [array((1024, width), bf16)] * 2,
        [VMEM] * 4 + [HBM] * len(given),
        12,
        scratch=[
            pltpu.VMEM((2, 256, width), bf16),
            pltpu.VMEM((2, 256, width), bf16),
            pltpu.SemaphoreType.DMA((4,)),
        ],
        out_specs=[HBM, HBM],
        input_output_aliases={4: 0, 5: 1} if given else {},
    )(x, left, rq, rk, *given)


def in_hbm(x):
    return pltpu.with_memory_space_constraint(x, pltpu.HBM)


def swapped(x, axis, bits):
    return lax.ppermute(x, axis, [(i, i ^ bits) for i in range(lax.axis_size(axis))])


def moved(x, axis, by):
    size = lax.axis_size(axis)
    return lax.ppermute(x, axis, [(i, (i + by) % size) for i in range(size)])


def per_device(
    features,
    block_gain,
    conv_weight,
    conv_bias,
    latent_weight,
    latent_bias,
    patch_weight,
    patch_bias,
    shift_mod,
    scale_mod,
    query_weight,
    query_bias,
    query_gain,
    key_weight,
    key_bias,
    key_gain,
    packing,
):
    channels = features.shape[-1]
    row = lambda v: v.reshape(1, -1)
    features, block_gain, conv_bias, lwt, latent_bias, conv_weight = map(
        in_hbm,
        (
            features.reshape(-1, channels),
            block_gain,
            conv_bias,
            latent_weight.T,
            latent_bias,
            conv_weight.reshape(27, channels, channels),
        ),
    )
    ahead, own, act = early_latents(
        features, block_gain, conv_bias, lwt, latent_bias, conv_weight
    )
    before = moved(ahead, "tm", 1)
    own = late_latents(own, act, lwt, conv_weight)
    copies = own_block(own, before)
    copies, patch_weight = lax.optimization_barrier((copies, patch_weight))
    plane = lax.all_to_all(copies, "rows", 0, 0, tiled=True)

    rq, rk, patch_gram, grams = weights_only(
        patch_weight,
        row(patch_bias),
        row(shift_mod),
        row(scale_mod),
        in_hbm(query_weight),
        in_hbm(key_weight),
        row(query_bias),
        row(key_bias),
        row(query_gain),
        row(key_gain),
    )
    grams = grams + swapped(grams, "tm", 1)
    plane, grams = lax.optimization_barrier((plane, grams))
    grams = grams + swapped(grams, "tm", 2) + swapped(grams, "tm", 4) + swapped(grams, "tm", 6)
    left = quadratic_forms(patch_gram, grams)

    keep, send = selected(packing, plane)
    mine = keep + swapped(send, "tm", 1)
    mine = mine + swapped(mine, "tm", 2) + swapped(mine, "tm", 4) + swapped(mine, "tm", 6)
    other = swapped(mine, "tm", 1)
    return tokens(other, left, rq, rk, tokens(mine, left, rq, rk))


def solution(mesh):
    in_specs = (
        P("tm", "rows", None, None),
        P(),
        P(),
        P(),
        P(),
        P(),
        P(),
        P(),
        P(),
        P(),
        P(None, "tm"),
        P("tm"),
        P("tm"),
        P(None, "tm"),
        P("tm"),
        P("tm"),
        P(),
    )
    out_specs = (P("rows", "tm"), P("rows", "tm"))
    return jax.shard_map(
        per_device, mesh=mesh, in_specs=in_specs, out_specs=out_specs, check_vma=False
    )
```

```python
import functools

import jax
import jax.numpy as jnp
from jax import lax
from jax.experimental import pallas as pl
from jax.experimental.pallas import tpu as pltpu
from jax.sharding import PartitionSpec as P

epsilon = 1e-06
bf16 = jnp.bfloat16
f32 = jnp.float32
VMEM = pl.BlockSpec(memory_space=pltpu.VMEM)
SMEM = pl.BlockSpec(memory_space=pltpu.SMEM)
HBM = pl.BlockSpec(memory_space=pltpu.HBM)
MIB = 1 << 20
EXT = 80


def mm(a, b, ca, cb):
    return lax.dot_general(a, b, (((ca,), (cb,)), ((), ())), preferred_element_type=f32)


def halves(x):
    high = x.astype(bf16)
    return high, (x - high.astype(f32)).astype(bf16)


def iota(shape, dim):
    return lax.broadcasted_iota(jnp.int32, shape, dim)


def call(kernel, name, out_shape, in_specs, limit, scratch=(), cost=None, **more):
    more.setdefault("out_specs", jax.tree.map(lambda _: VMEM, out_shape))
    return pl.pallas_call(
        kernel,
        out_shape=out_shape,
        in_specs=in_specs,
        scratch_shapes=list(scratch),
        compiler_params=pltpu.CompilerParams(vmem_limit_bytes=limit * MIB),
        cost_estimate=cost,
        name=name,
        **more,
    )


def array(shape, kind):
    return jax.ShapeDtypeStruct(shape, kind)


def folded(lwt, cw, wt, first, count, a):
    for k in range(first, first + count):
        high, low = halves(mm(lwt, cw[k], 1, 1))
        at = a * 288 + (k % 9) * 16
        wt[pl.ds(at, 16), :] = high
        wt[pl.ds(at + 144, 16), :] = low


def shifted_sum(by_e):
    lane = iota((16, 128), 1)
    left = jnp.where(lane == 0, 0.0, pltpu.roll(by_e[0], 1, 1))
    right = jnp.where(lane == 127, 0.0, pltpu.roll(by_e[2], 127, 1))
    return left + by_e[1] + right


def contributions(gts, fo, ro):
    by_e = []
    for e in range(3):
        total = None
        for f in range(2):
            for r in range(2):
                a, b = f + 2 - fo, r + 2 - ro
                if a not in gts or not 0 <= b < 3:
                    continue
                k, q = b * 3 + e, f * 2 + r
                part = (
                    gts[a][pl.ds(k * 16, 16), pl.ds(q * 128, 128)]
                    + gts[a][pl.ds(144 + k * 16, 16), pl.ds(q * 128, 128)]
                )
                total = part if total is None else total + part
        by_e.append(total)
    return shifted_sum(by_e)


def chunks_of(source, target, sems, start, count, size, first_sem):
    return [
        pltpu.make_async_copy(
            source.at[pl.ds(start + i * size, size)],
            target.at[pl.ds(i * size, size)],
            sems.at[first_sem + i],
        )
        for i in range(count)
    ]


def silu_normed(values, gain):
    mean = jnp.mean(values * values, axis=-1, keepdims=True)
    y = values * lax.rsqrt(mean + epsilon) * gain
    return (y / (1.0 + jnp.exp(-y))).astype(bf16)


def early_kernel(
    feat_hbm, gain_hbm, bias_hbm, lwt_hbm, lb_hbm, cw_hbm, ahead, own, act_out,
    feat, gain, bias, lwt_ref, lb, cw, wt, gt, sems,
):
    small = [
        pltpu.make_async_copy(a, b, sems.at[6 + i])
        for i, (a, b) in enumerate(
            (
                (feat_hbm, feat),
                (gain_hbm, gain),
                (bias_hbm, bias),
                (lwt_hbm, lwt_ref),
                (lb_hbm, lb),
            )
        )
    ]
    for c in small:
        c.start()
    copies = chunks_of(cw_hbm, cw, sems, 0, 6, 3, 0)
    for c in copies[:3]:
        c.start()
    for c in small:
        c.wait()
    lwt = lwt_ref[...]
    for i, c in enumerate(copies):
        if i < 4:
            at = pl.ds(i * 128, 128)
            act_out[at, :] = silu_normed(feat[at, :].astype(f32), gain[...].reshape(1, -1))
        c.wait()
        if i + 3 < len(copies):
            copies[i + 3].start()
        folded(lwt, cw, wt, i * 3, 3, i // 3)
        if i == 3:
            gt[pl.ds(0, 288), :] = mm(wt[pl.ds(0, 288), :], act_out[...], 1, 1)
    direct = mm(lwt, feat[...], 1, 1)
    const = jnp.sum(lwt.astype(f32) * bias[...].reshape(1, -1), axis=1, keepdims=True)
    const = const + jnp.transpose(lb[...].reshape(1, -1))
    gt[pl.ds(288, 288), :] = mm(wt[pl.ds(288, 288), :], act_out[...], 1, 1)
    gt0, gt1 = gt.at[pl.ds(0, 288)], gt.at[pl.ds(288, 288)]
    for ro in range(4):
        for fo in (2, 3):
            ahead[fo - 2, ro] = contributions({0: gt0, 1: gt1}, fo, ro)
        own[0, ro] = jnp.zeros((16, 128), f32)
        own[1, ro] = contributions({1: gt1}, 1, ro)
        if 1 <= ro < 3:
            for fo in range(2):
                q = fo * 2 + ro - 1
                own[fo, ro] += direct[:, q * 128 : (q + 1) * 128] + const


def early_latents(*args):
    return call(
        early_kernel,
        "early_latents",
        [array((2, 4, 16, 128), f32), array((2, 4, 16, 128), f32), array((512, 384), bf16)],
        [HBM] * 6,
        20,
        scratch=[
            pltpu.VMEM((512, 384), bf16),
            pltpu.VMEM((384,), f32),
            pltpu.VMEM((384,), f32),
            pltpu.VMEM((16, 384), bf16),
            pltpu.VMEM((16,), f32),
            pltpu.VMEM((18, 384, 384), bf16),
            pltpu.VMEM((576, 384), bf16),
            pltpu.VMEM((576, 512), f32),
            pltpu.SemaphoreType.DMA((11,)),
        ],
    )(*args)


def late_kernel(own, act, lwt_hbm, cw_hbm, out, lwt, cw, wt, gt, sems):
    small = pltpu.make_async_copy(lwt_hbm, lwt, sems.at[3])
    small.start()
    copies = chunks_of(cw_hbm, cw, sems, 18, 3, 3, 0)
    for c in copies:
        c.start()
    small.wait()
    for i, c in enumerate(copies):
        c.wait()
        folded(lwt[...], cw, wt, i * 3, 3, 0)
    gt[...] = mm(wt[...], act[...], 1, 1)
    for fo in range(2):
        for ro in range(4):
            out[fo, ro] = own[fo, ro] + contributions({2: gt}, fo, ro)


def late_latents(*args):
    return call(
        late_kernel,
        "late_latents",
        array((2, 4, 16, 128), f32),
        [VMEM] * 2 + [HBM] * 2,
        10,
        scratch=[
            pltpu.VMEM((16, 384), bf16),
            pltpu.VMEM((9, 384, 384), bf16),
            pltpu.VMEM((288, 384), bf16),
            pltpu.VMEM((288, 512), f32),
            pltpu.SemaphoreType.DMA((4,)),
        ],
        cost=pl.CostEstimate(flops=3 * 10**9, bytes_accessed=5 * 10**6, transcendentals=0),
    )(*args)


def weights_kernel(
    pw, pb, shift, scale, wq_hbm, wk_hbm, bq, bk, gq, gk,
    rq, rk, patch_gram, grams, wq, wk, parts, sems,
):
    width = pw.shape[1]
    chunk = width // 4
    copies = chunks_of(wq_hbm, wq, sems, 0, 4, chunk, 0)
    copies = copies + chunks_of(wk_hbm, wk, sems, 0, 4, chunk, 4)
    for c in copies[:3]:
        c.start()
    to, at = iota((64, 64), 0), iota((64, 64), 1)
    wanted = 4 * (to % 16) + 2 * ((to // 16) % 2) + to // 32
    order = jnp.where(at == wanted, 1.0, 0.0).astype(bf16)
    rows = mm(order, pw[...], 1, 0)
    rows = rows - jnp.mean(rows, axis=1, keepdims=True)
    const = pb[...] - jnp.mean(pb[...], axis=1, keepdims=True)
    const_tail = jnp.where(iota((16, width), 0) == 0, const, 0.0)
    centered = jnp.concatenate([rows, const_tail], axis=0)
    high, low = halves(centered)
    both = mm(jnp.concatenate([high, low], axis=0), high, 1, 1)
    cross = both[EXT:, :]
    patch_gram[...] = (both[:EXT, :] + cross + jnp.transpose(cross)) * (1.0 / width)
    scaled = centered * (1.0 + scale[...])
    high, low = halves(jnp.where(iota((EXT, width), 0) == 65, shift[...], scaled))
    parts[pl.ds(0, EXT), :] = high
    parts[pl.ds(EXT, EXT), :] = low
    found = []
    for n, (w, bias, gain, right) in enumerate(((wq, bq, gq, rq), (wk, bk, gk, rk))):
        both = None
        for i in range(4):
            copies[n * 4 + i].wait()
            if n * 4 + i + 3 < 8:
                copies[n * 4 + i + 3].start()
            at = pl.ds(i * chunk, chunk)
            part = mm(parts[:, at], w[at, :], 1, 0)
            both = part if both is None else both + part
        rows = both[:EXT, :] + both[EXT:, :]
        rows = rows + jnp.where(iota(rows.shape, 0) == 65, bias[...], 0.0)
        high, low = halves(rows)
        pairs = mm(jnp.concatenate([high, low], axis=0), high, 1, 1)
        cross = pairs[EXT:, :]
        found.append(pairs[:EXT, :] + cross + jnp.transpose(cross))
        high, low = halves(rows * gain[...])
        right[pl.ds(0, EXT), :] = high
        right[pl.ds(EXT, EXT), :] = high
        right[pl.ds(2 * EXT, EXT), :] = low
    i, j = iota((EXT, EXT), 0), iota((EXT, EXT), 1)
    diagonal = jnp.sum(jnp.where(i == j, found[1], 0.0), axis=1, keepdims=True)
    grams[:, :EXT] = jnp.where(i >= j, found[0], found[1])
    grams[:, EXT:] = jnp.broadcast_to(diagonal, (EXT, 128 - EXT))


def weights_only(pw, pb, shift, scale, wq, wk, bq, bk, gq, gk):
    width, part = wq.shape
    return call(
        weights_kernel,
        "weights_only",
        [
            array((3 * EXT, part), bf16),
            array((3 * EXT, part), bf16),
            array((EXT, EXT), f32),
            array((EXT, 128), f32),
        ],
        [VMEM] * 4 + [HBM] * 2 + [VMEM] * 4,
        36,
        scratch=[
            pltpu.VMEM((width, part), bf16),
            pltpu.VMEM((width, part), bf16),
            pltpu.VMEM((2 * EXT, width), bf16),
            pltpu.SemaphoreType.DMA((8,)),
        ],
        cost=pl.CostEstimate(
            flops=4 * 2 * EXT * width * part * 4, bytes_accessed=2 * width * part * 2, transcendentals=0
        ),
    )(pw, pb, shift, scale, wq, wk, bq, bk, gq, gk)


def block_kernel(own, before, out):
    first = jnp.where(lax.axis_index("tm") == 0, 0.0, 1.0)
    rows = []
    for ro in (1, 2, 3, 0):
        frames = [own[f, ro] + before[f, ro] * first for f in range(2)]
        rows.append(jnp.concatenate(frames, axis=1).astype(bf16))
    source, target = iota((256, 256), 0), iota((256, 256), 1)
    wanted = ((target // 64) % 2) * 128 + 2 * (target % 64) + target // 128
    pick = jnp.where(source == wanted, 1.0, 0.0).astype(bf16)
    spread = mm(jnp.concatenate(rows, axis=0), pick, 1, 0).astype(bf16)
    block = jnp.concatenate(
        [spread[:32, :128], spread[:32, 128:], spread[32:, :128], spread[32:, 128:]], axis=0
    )
    for i in range(out.shape[0]):
        out[i] = block


def own_block(own, before):
    return call(
        block_kernel, "own_block", array((lax.axis_size("rows"), 128, 128), bf16), [VMEM] * 2, 4
    )(own, before)


def select_kernel(packing, blocks, grams, keep, send):
    t, r = lax.axis_index("tm"), lax.axis_index("rows")
    last = blocks.shape[0] - 1
    core = t % 2
    upper = (iota((64, 128), 0) // 16) % 2 == 0
    for out, half in ((keep, core), (send, 1 - core)):
        for i in range(4):
            ident = packing[r * 8 + half * 4 + i]
            place = ident % 16
            here = jnp.where(ident // 16 == t, 1.0, 0.0)
            first = jnp.where(place == 0, 0.0, here)
            final = jnp.where(place == last, 0.0, here)
            own = blocks[place, pl.ds(0, 64)].astype(f32)
            above = blocks[jnp.maximum(place - 1, 0), pl.ds(64, 64)].astype(f32)
            below = blocks[jnp.minimum(place + 1, last), pl.ds(64, 64)].astype(f32)
            value = own * here + jnp.where(upper, above * first, below * final)
            out[pl.ds(i * 64, 64), :] = value.astype(bf16)
    send[pl.ds(256, EXT), :], send[pl.ds(256 + EXT, EXT), :] = halves(grams[...])


def selected(packing, blocks, grams):
    return call(
        select_kernel,
        "select_blocks",
        [array((256, 128), bf16), array((256 + 2 * EXT, 128), bf16)],
        [SMEM, VMEM, VMEM],
        4,
    )(packing, blocks, grams)


def sent_grams(sent):
    return sent[pl.ds(256, EXT), :].astype(f32) + sent[pl.ds(256 + EXT, EXT), :].astype(f32)


def pair_kernel(keep, grams, sent, pair, pair_grams):
    pair[pl.ds(0, 256), :] = keep[...] + sent[pl.ds(0, 256), :]
    total = grams[...] + sent_grams(sent)
    pair_grams[...] = total
    pair[pl.ds(256, EXT), :], pair[pl.ds(256 + EXT, EXT), :] = halves(total)


def paired(keep, grams, sent):
    return call(
        pair_kernel,
        "pair_sums",
        [array(sent.shape, bf16), array(grams.shape, f32)],
        [VMEM] * 3,
        4,
    )(keep, grams, sent)


def forms_kernel(patch_gram, pair, pair_grams, s1, s2, s3, mine, left):
    blocks, total = pair[pl.ds(0, 256), :], pair_grams[...]
    for sent in (s1, s2, s3):
        blocks = blocks + sent[pl.ds(0, 256), :]
        total = total + sent_grams(sent)
    mine[...] = blocks
    i, j = iota((EXT, EXT), 0), iota((EXT, EXT), 1)
    total = total * (1.0 / 5120.0)
    square = total[:, :EXT]
    gq = jnp.where(i > j, 2.0 * square, 0.0) + jnp.where(i == j, square, 0.0)
    gk = jnp.where(i > j, 2.0 * jnp.transpose(square), 0.0)
    gk = gk + jnp.where(i == j, total[:, EXT : EXT + 1], 0.0)
    left[pl.ds(0, EXT), :] = jnp.concatenate(halves(patch_gram[...]), axis=1)
    for n, g in enumerate((gq, gk)):
        end = jnp.sum(jnp.where((i == 65) & (j == 65), g, 0.0), keepdims=True)
        g = jnp.where((i == 66) & (j == 64), end, g)
        left[pl.ds((n + 1) * EXT, EXT), :] = jnp.concatenate(halves(g), axis=1)


def quadratic_forms(*args):
    return call(
        forms_kernel,
        "quadratic_forms",
        [array((256, 128), bf16), array((3 * EXT, 2 * EXT), bf16)],
        [VMEM] * 6,
        4,
    )(*args)


def token_rows(x_ref, part, left, rights):
    at = part * 128
    x = jnp.concatenate([x_ref[pl.ds(at, 64), :], x_ref[pl.ds(at + 64, 64), :]], axis=1)
    tail = iota((EXT - 64, 256), 0)
    xf = jnp.concatenate([x.astype(f32), jnp.where(tail == 0, 1.0, 0.0)], axis=0)
    xe = xf.astype(bf16)
    t = mm(left[...], jnp.concatenate([xe, xe], axis=0), 1, 0)
    spread = jnp.sum(t[:EXT] * xf, axis=0, keepdims=True)
    scale = lax.rsqrt(spread + epsilon)
    found = []
    for n, right in enumerate(rights):
        tn = t[(n + 1) * EXT : (n + 2) * EXT]
        squares = (
            scale * scale * jnp.sum(tn * xf, axis=0, keepdims=True)
            + scale * tn[65:66]
            + tn[66:67]
        )
        beta = lax.rsqrt(squares + epsilon)
        alpha = scale * beta
        y = xf * alpha + jnp.where(iota((EXT, 256), 0) == 65, beta, 0.0)
        high, low = halves(y)
        lhs = jnp.concatenate([high, low, high], axis=0)
        found.append(mm(lhs, right[...], 0, 0).astype(bf16))
    return found


def first_kernel(x_ref, left, rq, rk, q_out, k_out):
    for part in range(2):
        at = pl.ds(part * 256, 256)
        q_out[at, :], k_out[at, :] = token_rows(x_ref, part, left, (rq, rk))


def first_tokens(x, left, rq, rk):
    return call(
        first_kernel, "first_tokens", [array((512, rq.shape[1]), bf16)] * 2, [VMEM] * 4, 6
    )(x, left, rq, rk)


def rest_kernel(x_ref, left, rq, rk, q_first, k_first, q_out, k_out, q_buf, k_buf, sems):
    core = lax.axis_index("tm") % 2
    copies = []

    def send(source, target, at, size):
        at = pl.ds(pl.multiple_of(at, 256), size)
        c = pltpu.make_async_copy(source, target.at[at], sems.at[len(copies)])
        c.start()
        copies.append(c)

    send(q_first, q_out, core * 512, 512)
    send(k_first, k_out, core * 512, 512)
    for part in range(2):
        q_buf[part], k_buf[part] = token_rows(x_ref, part, left, (rq, rk))
        send(q_buf.at[part], q_out, (1 - core) * 512 + part * 256, 256)
        send(k_buf.at[part], k_out, (1 - core) * 512 + part * 256, 256)
    for c in copies:
        c.wait()


def all_tokens(x, left, rq, rk, q_first, k_first):
    width = rq.shape[1]
    return call(
        rest_kernel,
        "rest_tokens",
        [array((1024, width), bf16)] * 2,
        [VMEM] * 6,
        8,
        scratch=[
            pltpu.VMEM((2, 256, width), bf16),
            pltpu.VMEM((2, 256, width), bf16),
            pltpu.SemaphoreType.DMA((6,)),
        ],
        out_specs=[HBM, HBM],
    )(x, left, rq, rk, q_first, k_first)


def in_hbm(x):
    return pltpu.with_memory_space_constraint(x, pltpu.HBM)


def swapped(x, axis, bits):
    return lax.ppermute(x, axis, [(i, i ^ bits) for i in range(lax.axis_size(axis))])


def moved(x, axis, by):
    size = lax.axis_size(axis)
    return lax.ppermute(x, axis, [(i, (i + by) % size) for i in range(size)])


def per_device(
    features,
    block_gain,
    conv_weight,
    conv_bias,
    latent_weight,
    latent_bias,
    patch_weight,
    patch_bias,
    shift_mod,
    scale_mod,
    query_weight,
    query_bias,
    query_gain,
    key_weight,
    key_bias,
    key_gain,
    packing,
):
    channels = features.shape[-1]
    row = lambda v: v.reshape(1, -1)
    features, block_gain, conv_bias, lwt, latent_bias, conv_weight = map(
        in_hbm,
        (
            features.reshape(-1, channels),
            block_gain,
            conv_bias,
            latent_weight.T,
            latent_bias,
            conv_weight.reshape(27, channels, channels),
        ),
    )
    ahead, own, act = early_latents(
        features, block_gain, conv_bias, lwt, latent_bias, conv_weight
    )
    before = moved(ahead, "tm", 1)
    own = late_latents(own, act, lwt, conv_weight)
    copies = own_block(own, before)
    copies, patch_weight = lax.optimization_barrier((copies, patch_weight))
    plane = lax.all_to_all(copies, "rows", 0, 0, tiled=True)

    rq, rk, patch_gram, grams = weights_only(
        patch_weight,
        row(patch_bias),
        row(shift_mod),
        row(scale_mod),
        in_hbm(query_weight),
        in_hbm(key_weight),
        row(query_bias),
        row(key_bias),
        row(query_gain),
        row(key_gain),
    )
    plane, grams = lax.optimization_barrier((plane, grams))
    keep, send = selected(packing, plane, grams)
    pair, pair_grams = paired(keep, grams, swapped(send, "tm", 1))
    sent = [swapped(pair, "tm", bits) for bits in (2, 4, 6)]
    mine, left = quadratic_forms(patch_gram, pair, pair_grams, *sent)
    other = swapped(mine, "tm", 1)
    return all_tokens(other, left, rq, rk, *first_tokens(mine, left, rq, rk))


def solution(mesh):
    in_specs = (
        P("tm", "rows", None, None),
        P(),
        P(),
        P(),
        P(),
        P(),
        P(),
        P(),
        P(),
        P(),
        P(None, "tm"),
        P("tm"),
        P("tm"),
        P(None, "tm"),
        P("tm"),
        P("tm"),
        P(),
    )
    out_specs = (P("rows", "tm"), P("rows", "tm"))
    return jax.shard_map(
        per_device, mesh=mesh, in_specs=in_specs, out_specs=out_specs, check_vma=False
    )
```

```python
import functools

import jax
import jax.numpy as jnp
from jax import lax
from jax.experimental import pallas as pl
from jax.experimental.pallas import tpu as pltpu
from jax.sharding import PartitionSpec as P

epsilon = 1e-06
bf16 = jnp.bfloat16
f32 = jnp.float32
VMEM = pl.BlockSpec(memory_space=pltpu.VMEM)
SMEM = pl.BlockSpec(memory_space=pltpu.SMEM)
HBM = pl.BlockSpec(memory_space=pltpu.HBM)
MIB = 1 << 20
EXT = 80
GRAM = 48


def mm(a, b, ca, cb):
    return lax.dot_general(a, b, (((ca,), (cb,)), ((), ())), preferred_element_type=f32)


def halves(x):
    high = x.astype(bf16)
    return high, (x - high.astype(f32)).astype(bf16)


def iota(shape, dim):
    return lax.broadcasted_iota(jnp.int32, shape, dim)


def call(kernel, name, out_shape, in_specs, limit, scratch=(), cost=None, **more):
    more.setdefault("out_specs", jax.tree.map(lambda _: VMEM, out_shape))
    return pl.pallas_call(
        kernel,
        out_shape=out_shape,
        in_specs=in_specs,
        scratch_shapes=list(scratch),
        compiler_params=pltpu.CompilerParams(vmem_limit_bytes=limit * MIB),
        cost_estimate=cost,
        name=name,
        **more,
    )


def array(shape, kind):
    return jax.ShapeDtypeStruct(shape, kind)


def folded(lwt, cw, wt, first, count):
    for k in range(first, first + count):
        high, low = halves(mm(lwt, cw[k], 1, 1))
        at = (k // 9) * 288 + (k % 9) * 16
        wt[pl.ds(at, 16), :] = high
        wt[pl.ds(at + 144, 16), :] = low


def shifted_sum(by_e):
    lane = iota((16, 128), 1)
    left = jnp.where(lane == 0, 0.0, pltpu.roll(by_e[0], 1, 1))
    right = jnp.where(lane == 127, 0.0, pltpu.roll(by_e[2], 127, 1))
    return left + by_e[1] + right


def contributions(gts, fo, ro):
    by_e = []
    for e in range(3):
        total = None
        for f in range(2):
            for r in range(2):
                a, b = f + 2 - fo, r + 2 - ro
                if a not in gts or not 0 <= b < 3:
                    continue
                k, q = b * 3 + e, f * 2 + r
                part = (
                    gts[a][pl.ds(k * 16, 16), pl.ds(q * 128, 128)]
                    + gts[a][pl.ds(144 + k * 16, 16), pl.ds(q * 128, 128)]
                )
                total = part if total is None else total + part
        by_e.append(total)
    return shifted_sum(by_e)


def chunks_of(source, target, sems, start, count, size, first_sem):
    return [
        pltpu.make_async_copy(
            source.at[pl.ds(start + i * size, size)],
            target.at[pl.ds(i * size, size)],
            sems.at[first_sem + i],
        )
        for i in range(count)
    ]


def silu_normed(values, gain):
    mean = jnp.mean(values * values, axis=-1, keepdims=True)
    y = values * lax.rsqrt(mean + epsilon) * gain
    return (y / (1.0 + jnp.exp(-y))).astype(bf16)


def early_kernel(
    feat_hbm, gain_hbm, bias_hbm, lwt_hbm, lb_hbm, cw_hbm, ahead, own, act_out,
    feat, gain, bias, lwt_ref, lb, cw, wt, gt, sems,
):
    small = [
        pltpu.make_async_copy(a, b, sems.at[6 + i])
        for i, (a, b) in enumerate(
            (
                (feat_hbm, feat),
                (gain_hbm, gain),
                (bias_hbm, bias),
                (lwt_hbm, lwt_ref),
                (lb_hbm, lb),
            )
        )
    ]
    for c in small:
        c.start()
    copies = chunks_of(cw_hbm, cw, sems, 0, 3, 6, 0)
    for c in copies:
        c.start()
    for c in small:
        c.wait()
    lwt = lwt_ref[...]
    act_out[...] = silu_normed(feat[...].astype(f32), gain[...].reshape(1, -1))
    for i, c in enumerate(copies):
        c.wait()
        folded(lwt, cw, wt, i * 6, 6)
    gt[pl.ds(0, 288), :] = mm(wt[pl.ds(0, 288), :], act_out[...], 1, 1)
    direct = mm(lwt, feat[...], 1, 1)
    const = jnp.sum(lwt.astype(f32) * bias[...].reshape(1, -1), axis=1, keepdims=True)
    const = const + jnp.transpose(lb[...].reshape(1, -1))
    gt[pl.ds(288, 288), :] = mm(wt[pl.ds(288, 288), :], act_out[...], 1, 1)
    gt0, gt1 = gt.at[pl.ds(0, 288)], gt.at[pl.ds(288, 288)]
    for ro in range(4):
        for fo in (2, 3):
            ahead[fo - 2, ro] = contributions({0: gt0, 1: gt1}, fo, ro)
        own[0, ro] = jnp.zeros((16, 128), f32)
        own[1, ro] = contributions({1: gt1}, 1, ro)
        if 1 <= ro < 3:
            for fo in range(2):
                q = fo * 2 + ro - 1
                own[fo, ro] += direct[:, q * 128 : (q + 1) * 128] + const


def early_latents(*args):
    return call(
        early_kernel,
        "early_latents",
        [array((2, 4, 16, 128), f32), array((2, 4, 16, 128), f32), array((512, 384), bf16)],
        [HBM] * 6,
        20,
        scratch=[
            pltpu.VMEM((512, 384), bf16),
            pltpu.VMEM((384,), f32),
            pltpu.VMEM((384,), f32),
            pltpu.VMEM((16, 384), bf16),
            pltpu.VMEM((16,), f32),
            pltpu.VMEM((18, 384, 384), bf16),
            pltpu.VMEM((576, 384), bf16),
            pltpu.VMEM((576, 512), f32),
            pltpu.SemaphoreType.DMA((11,)),
        ],
    )(*args)


def late_kernel(own, act, lwt_hbm, cw_hbm, out, lwt, cw, wt, gt, sems):
    small = pltpu.make_async_copy(lwt_hbm, lwt, sems.at[3])
    small.start()
    copies = chunks_of(cw_hbm, cw, sems, 18, 3, 3, 0)
    for c in copies:
        c.start()
    small.wait()
    for i, c in enumerate(copies):
        c.wait()
        folded(lwt[...], cw, wt, i * 3, 3)
    gt[...] = mm(wt[...], act[...], 1, 1)
    for fo in range(2):
        for ro in range(4):
            out[fo, ro] = own[fo, ro] + contributions({2: gt}, fo, ro)


def late_latents(*args):
    return call(
        late_kernel,
        "late_latents",
        array((2, 4, 16, 128), f32),
        [VMEM] * 2 + [HBM] * 2,
        10,
        scratch=[
            pltpu.VMEM((16, 384), bf16),
            pltpu.VMEM((9, 384, 384), bf16),
            pltpu.VMEM((288, 384), bf16),
            pltpu.VMEM((288, 512), f32),
            pltpu.SemaphoreType.DMA((4,)),
        ],
        cost=pl.CostEstimate(flops=3 * 10**9, bytes_accessed=5 * 10**6, transcendentals=0),
    )(*args)


def weights_kernel(
    pw, pb, shift, scale, wq_hbm, wk_hbm, bq, bk, gq, gk,
    rq, rk, last, patch_gram, grams, wq, wk, parts, sems,
):
    width = pw.shape[1]
    chunk = width // 4
    copies = chunks_of(wq_hbm, wq, sems, 0, 4, chunk, 0)
    copies = copies + chunks_of(wk_hbm, wk, sems, 0, 4, chunk, 4)
    for c in copies[:3]:
        c.start()
    to, at = iota((64, 64), 0), iota((64, 64), 1)
    wanted = 4 * (to % 16) + 2 * ((to // 16) % 2) + to // 32
    order = jnp.where(at == wanted, 1.0, 0.0).astype(bf16)
    rows = mm(order, pw[...], 1, 0)
    rows = rows - jnp.mean(rows, axis=1, keepdims=True)
    const = pb[...] - jnp.mean(pb[...], axis=1, keepdims=True)
    const_tail = jnp.where(iota((16, width), 0) == 0, const, 0.0)
    centered = jnp.concatenate([rows, const_tail], axis=0)
    high, low = halves(centered)
    both = mm(jnp.concatenate([high, low], axis=0), high, 1, 1)
    cross = both[EXT:, :]
    patch_gram[...] = (both[:EXT, :] + cross + jnp.transpose(cross)) * (1.0 / width)
    scaled = centered * (1.0 + scale[...])
    high, low = halves(jnp.where(iota((EXT, width), 0) == 65, shift[...], scaled))
    parts[pl.ds(0, EXT), :] = high
    parts[pl.ds(EXT, EXT), :] = low
    found = []
    for n, (w, bias, gain, right) in enumerate(((wq, bq, gq, rq), (wk, bk, gk, rk))):
        both = None
        for i in range(4):
            copies[n * 4 + i].wait()
            if n * 4 + i + 3 < 8:
                copies[n * 4 + i + 3].start()
            at = pl.ds(i * chunk, chunk)
            part = mm(parts[:, at], w[at, :], 1, 0)
            both = part if both is None else both + part
        rows = both[:EXT, :] + both[EXT:, :]
        rows = rows + jnp.where(iota(rows.shape, 0) == 65, bias[...], 0.0)
        high, low = halves(rows)
        pairs = mm(jnp.concatenate([high, low], axis=0), high, 1, 1)
        cross = pairs[EXT:, :]
        found.append(pairs[:EXT, :] + cross + jnp.transpose(cross))
        rows = rows * gain[...]
        shifted = iota(rows.shape, 0) == 65
        high, low = halves(jnp.where(shifted, 0.0, rows))
        right[pl.ds(0, EXT), :] = high
        right[pl.ds(EXT, EXT), :] = low
        last[n : n + 1, :] = jnp.sum(jnp.where(shifted, rows, 0.0), axis=0, keepdims=True)
    i, j = iota((EXT, EXT), 0), iota((EXT, EXT), 1)
    square = jnp.where(i >= j, found[0], found[1])
    grams[pl.ds(0, 32), :] = jnp.concatenate([square[:32, :64], square[32:64, :64]], axis=1)
    grams[pl.ds(32, 16), :] = jnp.zeros((16, 128), f32)
    grams[pl.ds(32, 2), pl.ds(0, EXT)] = found[0][64:66]
    grams[pl.ds(34, 2), pl.ds(0, EXT)] = found[1][64:66]
    diagonal = jnp.sum(jnp.where(i == j, found[1], 0.0), axis=0, keepdims=True)
    grams[pl.ds(36, 1), pl.ds(0, EXT)] = diagonal


def weights_only(pw, pb, shift, scale, wq, wk, bq, bk, gq, gk):
    width, part = wq.shape
    return call(
        weights_kernel,
        "weights_only",
        [
            array((2 * EXT, part), bf16),
            array((2 * EXT, part), bf16),
            array((8, part), f32),
            array((EXT, EXT), f32),
            array((GRAM, 128), f32),
        ],
        [VMEM] * 4 + [HBM] * 2 + [VMEM] * 4,
        36,
        scratch=[
            pltpu.VMEM((width, part), bf16),
            pltpu.VMEM((width, part), bf16),
            pltpu.VMEM((2 * EXT, width), bf16),
            pltpu.SemaphoreType.DMA((8,)),
        ],
        cost=pl.CostEstimate(
            flops=4 * 2 * EXT * width * part * 4, bytes_accessed=2 * width * part * 2, transcendentals=0
        ),
    )(pw, pb, shift, scale, wq, wk, bq, bk, gq, gk)


def block_kernel(own, before, out):
    first = jnp.where(lax.axis_index("tm") == 0, 0.0, 1.0)
    rows = []
    for ro in (1, 2, 3, 0):
        frames = [own[f, ro] + before[f, ro] * first for f in range(2)]
        rows.append(jnp.concatenate(frames, axis=1).astype(bf16))
    source, target = iota((256, 256), 0), iota((256, 256), 1)
    wanted = ((target // 64) % 2) * 128 + 2 * (target % 64) + target // 128
    pick = jnp.where(source == wanted, 1.0, 0.0).astype(bf16)
    spread = mm(jnp.concatenate(rows, axis=0), pick, 1, 0).astype(bf16)
    block = jnp.concatenate(
        [spread[:32, :128], spread[:32, 128:], spread[32:, :128], spread[32:, 128:]], axis=0
    )
    for i in range(out.shape[0]):
        out[i] = block


def own_block(own, before):
    return call(
        block_kernel, "own_block", array((lax.axis_size("rows"), 128, 128), bf16), [VMEM] * 2, 4
    )(own, before)


SLOTS = 256
SENT = SLOTS + 2 * GRAM


def select_kernel(packing, blocks, grams, keep, send):
    t, r = lax.axis_index("tm"), lax.axis_index("rows")
    last = blocks.shape[0] - 1
    core = t % 2
    upper = (iota((64, 128), 0) // 16) % 2 == 0
    for out, half in ((keep, core), (send, 1 - core)):
        for i in range(4):
            ident = packing[r * 8 + half * 4 + i]
            place = ident % 16
            here = jnp.where(ident // 16 == t, 1.0, 0.0)
            first = jnp.where(place == 0, 0.0, here)
            final = jnp.where(place == last, 0.0, here)
            own = blocks[place, pl.ds(0, 64)].astype(f32)
            above = blocks[jnp.maximum(place - 1, 0), pl.ds(64, 64)].astype(f32)
            below = blocks[jnp.minimum(place + 1, last), pl.ds(64, 64)].astype(f32)
            value = own * here + jnp.where(upper, above * first, below * final)
            out[pl.ds(i * 64, 64), :] = value.astype(bf16)
    send[pl.ds(SLOTS, GRAM), :], send[pl.ds(SLOTS + GRAM, GRAM), :] = halves(grams[...])


def selected(packing, blocks, grams):
    return call(
        select_kernel,
        "select_blocks",
        [array((SLOTS, 128), bf16), array((SENT, 128), bf16)],
        [SMEM, VMEM, VMEM],
        4,
    )(packing, blocks, grams)


def sent_grams(sent):
    return sent[pl.ds(SLOTS, GRAM), :].astype(f32) + sent[pl.ds(SLOTS + GRAM, GRAM), :].astype(f32)


def add_kernel(own, grams, sent, out, out_grams):
    slots = pl.ds(0, SLOTS)
    out[slots, :] = own[slots, :] + sent[slots, :]
    total = grams[...] + sent_grams(sent)
    out_grams[...] = total
    out[pl.ds(SLOTS, GRAM), :], out[pl.ds(SLOTS + GRAM, GRAM), :] = halves(total)


def added(own, grams, sent):
    return call(
        add_kernel,
        "add_sums",
        [array((SENT, 128), bf16), array(grams.shape, f32)],
        [VMEM] * 3,
        4,
    )(own, grams, sent)


def quadratic_forms(patch_gram, total):
    total = total * (1.0 / 5120.0)
    i, j = iota((64, 64), 0), iota((64, 64), 1)
    square = jnp.concatenate([total[:32, :64], total[:32, 64:]], axis=0)
    turned = jnp.transpose(square)
    squares = (
        jnp.where(i > j, 2.0 * square, jnp.where(i == j, square, 0.0)),
        jnp.where(i > j, 2.0 * turned, jnp.where(i == j, total[36:37, :64], 0.0)),
    )
    row, lane = iota((EXT - 64, EXT), 0), iota((EXT - 64, EXT), 1)
    forms = [jnp.concatenate(halves(patch_gram), axis=1)]
    for n, g in enumerate(squares):
        const = total[32 + 2 * n : 33 + 2 * n, :EXT]
        shift = total[33 + 2 * n : 34 + 2 * n, :EXT]
        end = total[33 + 2 * n : 34 + 2 * n, 65:66]
        below = jnp.where(lane < 64, 2.0 * const, jnp.where(lane == 64, const, 0.0))
        linear = jnp.where(lane <= 64, 2.0 * shift, 0.0)
        last = jnp.where(lane == 64, end, 0.0)
        below = jnp.where(row == 0, below, jnp.where(row == 1, linear, 0.0))
        below = jnp.where(row == 2, last, below)
        g = jnp.concatenate([g, jnp.zeros((64, EXT - 64), f32)], axis=1)
        g = jnp.concatenate([g, below], axis=0)
        forms.append(jnp.concatenate(halves(g), axis=1))
    return jnp.concatenate(forms, axis=0)


def total_kernel(patch_gram, own, own_grams, s1, s2, s3, mine, forms):
    slots = pl.ds(0, SLOTS)
    mine[...] = own[slots, :] + s1[slots, :] + s2[slots, :] + s3[slots, :]
    total = own_grams[...] + sent_grams(s1) + sent_grams(s2) + sent_grams(s3)
    forms[...] = quadratic_forms(patch_gram[...], total)


def totals(*args):
    return call(
        total_kernel,
        "total_sums",
        [array((SLOTS, 128), bf16), array((3 * EXT, 2 * EXT), bf16)],
        [VMEM] * 6,
        4,
    )(*args)


def token_rows(x_ref, part, forms, rights, last):
    at = part * 128
    x = jnp.concatenate([x_ref[pl.ds(at, 64), :], x_ref[pl.ds(at + 64, 64), :]], axis=1)
    tail = jnp.where(iota((EXT - 64, 256), 0) == 0, 1.0, 0.0)
    xf = jnp.concatenate([x.astype(f32), tail], axis=0)
    xe = xf.astype(bf16)
    lhs = jnp.transpose(xf).astype(bf16)
    lhs = jnp.concatenate([lhs, lhs], axis=1)
    t = mm(forms[...], jnp.concatenate([xe, xe], axis=0), 1, 0)
    scale = lax.rsqrt(jnp.sum(t[:EXT] * xf, axis=0, keepdims=True) + epsilon)
    row = iota((8, 256), 0)
    stacked = jnp.zeros((8, 256), f32)
    for n in range(2):
        tn = t[(n + 1) * EXT : (n + 2) * EXT]
        squares = (
            scale * scale * jnp.sum(tn * xf, axis=0, keepdims=True)
            + scale * tn[65:66]
            + tn[66:67]
        )
        beta = lax.rsqrt(squares + epsilon)
        stacked = jnp.where(row == 2 * n, scale * beta, stacked)
        stacked = jnp.where(row == 2 * n + 1, beta, stacked)
    columns = jnp.transpose(stacked)
    found = []
    for n, right in enumerate(rights):
        alpha, beta = columns[:, 2 * n : 2 * n + 1], columns[:, 2 * n + 1 : 2 * n + 2]
        value = mm(lhs, right[...], 1, 0) * alpha + beta * last[n : n + 1, :]
        found.append(value.astype(bf16))
    return found


def first_kernel(x_ref, forms, rq, rk, last, q_out, k_out):
    for part in range(2):
        at = pl.ds(part * 256, 256)
        q_out[at, :], k_out[at, :] = token_rows(x_ref, part, forms, (rq, rk), last)


def first_tokens(x, forms, rq, rk, last):
    return call(
        first_kernel, "first_tokens", [array((512, rq.shape[1]), bf16)] * 2, [VMEM] * 5, 6
    )(x, forms, rq, rk, last)


def rest_kernel(
    x_ref, forms, rq, rk, last, q_first, k_first, q_out, k_out, q_buf, k_buf, sems
):
    core = lax.axis_index("tm") % 2
    copies = []

    def send(source, target, at, size):
        at = pl.ds(pl.multiple_of(at, 256), size)
        c = pltpu.make_async_copy(source, target.at[at], sems.at[len(copies)])
        c.start()
        copies.append(c)

    send(q_first, q_out, core * 512, 512)
    send(k_first, k_out, core * 512, 512)
    for part in range(2):
        q_buf[part], k_buf[part] = token_rows(x_ref, part, forms, (rq, rk), last)
        send(q_buf.at[part], q_out, (1 - core) * 512 + part * 256, 256)
        send(k_buf.at[part], k_out, (1 - core) * 512 + part * 256, 256)
    for c in copies:
        c.wait()


def all_tokens(x, forms, rq, rk, last, q_first, k_first):
    width = rq.shape[1]
    return call(
        rest_kernel,
        "rest_tokens",
        [array((1024, width), bf16)] * 2,
        [VMEM] * 7,
        8,
        scratch=[
            pltpu.VMEM((2, 256, width), bf16),
            pltpu.VMEM((2, 256, width), bf16),
            pltpu.SemaphoreType.DMA((6,)),
        ],
        out_specs=[HBM, HBM],
    )(x, forms, rq, rk, last, q_first, k_first)


def in_hbm(x):
    return pltpu.with_memory_space_constraint(x, pltpu.HBM)


def swapped(x, axis, bits):
    return lax.ppermute(x, axis, [(i, i ^ bits) for i in range(lax.axis_size(axis))])


def by_core(x, axis, bits0, bits1):
    route = [(i, i ^ (bits1 if i % 2 else bits0)) for i in range(lax.axis_size(axis))]
    return lax.ppermute(x, axis, route)


def moved(x, axis, by):
    size = lax.axis_size(axis)
    return lax.ppermute(x, axis, [(i, (i + by) % size) for i in range(size)])


def per_device(
    features,
    block_gain,
    conv_weight,
    conv_bias,
    latent_weight,
    latent_bias,
    patch_weight,
    patch_bias,
    shift_mod,
    scale_mod,
    query_weight,
    query_bias,
    query_gain,
    key_weight,
    key_bias,
    key_gain,
    packing,
):
    channels = features.shape[-1]
    row = lambda v: v.reshape(1, -1)
    features, block_gain, conv_bias, lwt, latent_bias, conv_weight = map(
        in_hbm,
        (
            features.reshape(-1, channels),
            block_gain,
            conv_bias,
            latent_weight.T,
            latent_bias,
            conv_weight.reshape(27, channels, channels),
        ),
    )
    ahead, own, act = early_latents(
        features, block_gain, conv_bias, lwt, latent_bias, conv_weight
    )
    before = moved(ahead, "tm", 1)
    own = late_latents(own, act, lwt, conv_weight)
    copies = own_block(own, before)
    copies, patch_weight = lax.optimization_barrier((copies, patch_weight))
    plane = lax.all_to_all(copies, "rows", 0, 0, tiled=True)

    rq, rk, last, patch_gram, grams = weights_only(
        patch_weight,
        row(patch_bias),
        row(shift_mod),
        row(scale_mod),
        in_hbm(query_weight),
        in_hbm(key_weight),
        row(query_bias),
        row(key_bias),
        row(query_gain),
        row(key_gain),
    )
    plane, grams = lax.optimization_barrier((plane, grams))
    keep, send = selected(packing, plane, grams)
    own, grams = added(keep, grams, swapped(send, "tm", 1))
    sent = [swapped(own, "tm", bits) for bits in (2, 4, 6)]
    mine, forms = totals(patch_gram, own, grams, *sent)
    first = first_tokens(mine, forms, rq, rk, last)
    return all_tokens(swapped(mine, "tm", 1), forms, rq, rk, last, *first)


def solution(mesh):
    in_specs = (
        P("tm", "rows", None, None),
        P(),
        P(),
        P(),
        P(),
        P(),
        P(),
        P(),
        P(),
        P(),
        P(None, "tm"),
        P("tm"),
        P("tm"),
        P(None, "tm"),
        P("tm"),
        P("tm"),
        P(),
    )
    out_specs = (P("rows", "tm"), P("rows", "tm"))
    return jax.shard_map(
        per_device, mesh=mesh, in_specs=in_specs, out_specs=out_specs, check_vma=False
    )
```

```python
import functools

import jax
import jax.numpy as jnp
from jax import lax
from jax.experimental import pallas as pl
from jax.experimental.pallas import tpu as pltpu
from jax.sharding import PartitionSpec as P

epsilon = 1e-06
bf16 = jnp.bfloat16
f32 = jnp.float32
VMEM = pl.BlockSpec(memory_space=pltpu.VMEM)
SMEM = pl.BlockSpec(memory_space=pltpu.SMEM)
HBM = pl.BlockSpec(memory_space=pltpu.HBM)
MIB = 1 << 20
EXT = 80
GRAM = 48


def mm(a, b, ca, cb):
    return lax.dot_general(a, b, (((ca,), (cb,)), ((), ())), preferred_element_type=f32)


def halves(x):
    high = x.astype(bf16)
    return high, (x - high.astype(f32)).astype(bf16)


def iota(shape, dim):
    return lax.broadcasted_iota(jnp.int32, shape, dim)


def call(kernel, name, out_shape, in_specs, limit, scratch=(), cost=None, **more):
    more.setdefault("out_specs", jax.tree.map(lambda _: VMEM, out_shape))
    return pl.pallas_call(
        kernel,
        out_shape=out_shape,
        in_specs=in_specs,
        scratch_shapes=list(scratch),
        compiler_params=pltpu.CompilerParams(vmem_limit_bytes=limit * MIB),
        cost_estimate=cost,
        name=name,
        **more,
    )


def array(shape, kind):
    return jax.ShapeDtypeStruct(shape, kind)


def folded(lwt, cw, wt, first, count):
    for k in range(first, first + count):
        high, low = halves(mm(lwt, cw[k], 1, 1))
        at = (k // 9) * 288 + (k % 9) * 16
        wt[pl.ds(at, 16), :] = high
        wt[pl.ds(at + 144, 16), :] = low


def shifted_sum(by_e):
    lane = iota((16, 128), 1)
    left = jnp.where(lane == 0, 0.0, pltpu.roll(by_e[0], 1, 1))
    right = jnp.where(lane == 127, 0.0, pltpu.roll(by_e[2], 127, 1))
    return left + by_e[1] + right


def contributions(gts, fo, ro):
    by_e = []
    for e in range(3):
        total = None
        for f in range(2):
            for r in range(2):
                a, b = f + 2 - fo, r + 2 - ro
                if a not in gts or not 0 <= b < 3:
                    continue
                k, q = b * 3 + e, f * 2 + r
                part = (
                    gts[a][pl.ds(k * 16, 16), pl.ds(q * 128, 128)]
                    + gts[a][pl.ds(144 + k * 16, 16), pl.ds(q * 128, 128)]
                )
                total = part if total is None else total + part
        by_e.append(total)
    return shifted_sum(by_e)


def chunks_of(source, target, sems, start, count, size, first_sem):
    return [
        pltpu.make_async_copy(
            source.at[pl.ds(start + i * size, size)],
            target.at[pl.ds(i * size, size)],
            sems.at[first_sem + i],
        )
        for i in range(count)
    ]


def silu_normed(values, gain):
    mean = jnp.mean(values * values, axis=-1, keepdims=True)
    y = values * lax.rsqrt(mean + epsilon) * gain
    return (y / (1.0 + jnp.exp(-y))).astype(bf16)


def early_kernel(
    feat_hbm, gain_hbm, bias_hbm, lwt_hbm, lb_hbm, cw_hbm, ahead, own, act_out,
    feat, gain, bias, lwt_ref, lb, cw, wt, gt, sems,
):
    small = [
        pltpu.make_async_copy(a, b, sems.at[6 + i])
        for i, (a, b) in enumerate(
            (
                (feat_hbm, feat),
                (gain_hbm, gain),
                (bias_hbm, bias),
                (lwt_hbm, lwt_ref),
                (lb_hbm, lb),
            )
        )
    ]
    for c in small:
        c.start()
    copies = chunks_of(cw_hbm, cw, sems, 0, 3, 6, 0)
    for c in copies:
        c.start()
    for c in small:
        c.wait()
    lwt = lwt_ref[...]
    act_out[...] = silu_normed(feat[...].astype(f32), gain[...].reshape(1, -1))
    for i, c in enumerate(copies):
        c.wait()
        folded(lwt, cw, wt, i * 6, 6)
    gt[pl.ds(0, 288), :] = mm(wt[pl.ds(0, 288), :], act_out[...], 1, 1)
    direct = mm(lwt, feat[...], 1, 1)
    const = jnp.sum(lwt.astype(f32) * bias[...].reshape(1, -1), axis=1, keepdims=True)
    const = const + jnp.transpose(lb[...].reshape(1, -1))
    gt[pl.ds(288, 288), :] = mm(wt[pl.ds(288, 288), :], act_out[...], 1, 1)
    gt0, gt1 = gt.at[pl.ds(0, 288)], gt.at[pl.ds(288, 288)]
    for ro in range(4):
        for fo in (2, 3):
            ahead[fo - 2, ro] = contributions({0: gt0, 1: gt1}, fo, ro)
        own[0, ro] = jnp.zeros((16, 128), f32)
        own[1, ro] = contributions({1: gt1}, 1, ro)
        if 1 <= ro < 3:
            for fo in range(2):
                q = fo * 2 + ro - 1
                own[fo, ro] += direct[:, q * 128 : (q + 1) * 128] + const


def early_latents(*args):
    return call(
        early_kernel,
        "early_latents",
        [array((2, 4, 16, 128), f32), array((2, 4, 16, 128), f32), array((512, 384), bf16)],
        [HBM] * 6,
        20,
        scratch=[
            pltpu.VMEM((512, 384), bf16),
            pltpu.VMEM((384,), f32),
            pltpu.VMEM((384,), f32),
            pltpu.VMEM((16, 384), bf16),
            pltpu.VMEM((16,), f32),
            pltpu.VMEM((18, 384, 384), bf16),
            pltpu.VMEM((576, 384), bf16),
            pltpu.VMEM((576, 512), f32),
            pltpu.SemaphoreType.DMA((11,)),
        ],
    )(*args)


def late_kernel(own, act, lwt_hbm, cw_hbm, out, lwt, cw, wt, gt, sems):
    small = pltpu.make_async_copy(lwt_hbm, lwt, sems.at[3])
    small.start()
    copies = chunks_of(cw_hbm, cw, sems, 18, 3, 3, 0)
    for c in copies:
        c.start()
    small.wait()
    for i, c in enumerate(copies):
        c.wait()
        folded(lwt[...], cw, wt, i * 3, 3)
    gt[...] = mm(wt[...], act[...], 1, 1)
    for fo in range(2):
        for ro in range(4):
            out[fo, ro] = own[fo, ro] + contributions({2: gt}, fo, ro)


def late_latents(*args):
    return call(
        late_kernel,
        "late_latents",
        array((2, 4, 16, 128), f32),
        [VMEM] * 2 + [HBM] * 2,
        10,
        scratch=[
            pltpu.VMEM((16, 384), bf16),
            pltpu.VMEM((9, 384, 384), bf16),
            pltpu.VMEM((288, 384), bf16),
            pltpu.VMEM((288, 512), f32),
            pltpu.SemaphoreType.DMA((4,)),
        ],
        cost=pl.CostEstimate(flops=3 * 10**9, bytes_accessed=5 * 10**6, transcendentals=0),
    )(*args)


def weights_kernel(
    pw, pb, shift, scale, wq_hbm, wk_hbm, bq, bk, gq, gk,
    rq, rk, last, patch_gram, grams, wq, wk, parts, sems,
):
    width = pw.shape[1]
    chunk = width // 4
    copies = chunks_of(wq_hbm, wq, sems, 0, 4, chunk, 0)
    copies = copies + chunks_of(wk_hbm, wk, sems, 0, 4, chunk, 4)
    for c in copies[:3]:
        c.start()
    to, at = iota((64, 64), 0), iota((64, 64), 1)
    wanted = 4 * (to % 16) + 2 * ((to // 16) % 2) + to // 32
    order = jnp.where(at == wanted, 1.0, 0.0).astype(bf16)
    rows = mm(order, pw[...], 1, 0)
    rows = rows - jnp.mean(rows, axis=1, keepdims=True)
    const = pb[...] - jnp.mean(pb[...], axis=1, keepdims=True)
    const_tail = jnp.where(iota((16, width), 0) == 0, const, 0.0)
    centered = jnp.concatenate([rows, const_tail], axis=0)
    high, low = halves(centered)
    both = mm(jnp.concatenate([high, low], axis=0), high, 1, 1)
    cross = both[EXT:, :]
    patch_gram[...] = (both[:EXT, :] + cross + jnp.transpose(cross)) * (1.0 / width)
    scaled = centered * (1.0 + scale[...])
    high, low = halves(jnp.where(iota((EXT, width), 0) == 65, shift[...], scaled))
    parts[pl.ds(0, EXT), :] = high
    parts[pl.ds(EXT, EXT), :] = low
    found = []
    for n, (w, bias, gain, right) in enumerate(((wq, bq, gq, rq), (wk, bk, gk, rk))):
        both = None
        for i in range(4):
            copies[n * 4 + i].wait()
            if n * 4 + i + 3 < 8:
                copies[n * 4 + i + 3].start()
            at = pl.ds(i * chunk, chunk)
            part = mm(parts[:, at], w[at, :], 1, 0)
            both = part if both is None else both + part
        rows = both[:EXT, :] + both[EXT:, :]
        rows = rows + jnp.where(iota(rows.shape, 0) == 65, bias[...], 0.0)
        high, low = halves(rows)
        pairs = mm(jnp.concatenate([high, low], axis=0), high, 1, 1)
        cross = pairs[EXT:, :]
        found.append(pairs[:EXT, :] + cross + jnp.transpose(cross))
        rows = rows * gain[...]
        shifted = iota(rows.shape, 0) == 65
        high, low = halves(jnp.where(shifted, 0.0, rows))
        right[pl.ds(0, EXT), :] = high
        right[pl.ds(EXT, EXT), :] = low
        last[n : n + 1, :] = jnp.sum(jnp.where(shifted, rows, 0.0), axis=0, keepdims=True)
    i, j = iota((EXT, EXT), 0), iota((EXT, EXT), 1)
    square = jnp.where(i >= j, found[0], found[1])
    grams[pl.ds(0, 32), :] = jnp.concatenate([square[:32, :64], square[32:64, :64]], axis=1)
    grams[pl.ds(32, 16), :] = jnp.zeros((16, 128), f32)
    grams[pl.ds(32, 2), pl.ds(0, EXT)] = found[0][64:66]
    grams[pl.ds(34, 2), pl.ds(0, EXT)] = found[1][64:66]
    diagonal = jnp.sum(jnp.where(i == j, found[1], 0.0), axis=0, keepdims=True)
    grams[pl.ds(36, 1), pl.ds(0, EXT)] = diagonal


def weights_only(pw, pb, shift, scale, wq, wk, bq, bk, gq, gk):
    width, part = wq.shape
    return call(
        weights_kernel,
        "weights_only",
        [
            array((2 * EXT, part), bf16),
            array((2 * EXT, part), bf16),
            array((8, part), f32),
            array((EXT, EXT), f32),
            array((GRAM, 128), f32),
        ],
        [VMEM] * 4 + [HBM] * 2 + [VMEM] * 4,
        36,
        scratch=[
            pltpu.VMEM((width, part), bf16),
            pltpu.VMEM((width, part), bf16),
            pltpu.VMEM((2 * EXT, width), bf16),
            pltpu.SemaphoreType.DMA((8,)),
        ],
        cost=pl.CostEstimate(
            flops=4 * 2 * EXT * width * part * 4, bytes_accessed=2 * width * part * 2, transcendentals=0
        ),
    )(pw, pb, shift, scale, wq, wk, bq, bk, gq, gk)


def block_kernel(own, before, out):
    first = jnp.where(lax.axis_index("tm") == 0, 0.0, 1.0)
    rows = []
    for ro in (1, 2, 3, 0):
        frames = [own[f, ro] + before[f, ro] * first for f in range(2)]
        rows.append(jnp.concatenate(frames, axis=1).astype(bf16))
    source, target = iota((256, 256), 0), iota((256, 256), 1)
    wanted = ((target // 64) % 2) * 128 + 2 * (target % 64) + target // 128
    pick = jnp.where(source == wanted, 1.0, 0.0).astype(bf16)
    spread = mm(jnp.concatenate(rows, axis=0), pick, 1, 0).astype(bf16)
    block = jnp.concatenate(
        [spread[:32, :128], spread[:32, 128:], spread[32:, :128], spread[32:, 128:]], axis=0
    )
    for i in range(out.shape[0]):
        out[i] = block


def own_block(own, before):
    return call(
        block_kernel, "own_block", array((lax.axis_size("rows"), 128, 128), bf16), [VMEM] * 2, 4
    )(own, before)


SLOTS = 256
SENT = SLOTS + 2 * GRAM


def select_kernel(packing, blocks, grams, keep, send):
    t, r = lax.axis_index("tm"), lax.axis_index("rows")
    last = blocks.shape[0] - 1
    core = t % 2
    upper = (iota((64, 128), 0) // 16) % 2 == 0
    for out, half in ((keep, core), (send, 1 - core)):
        for i in range(4):
            ident = packing[r * 8 + half * 4 + i]
            place = ident % 16
            here = jnp.where(ident // 16 == t, 1.0, 0.0)
            first = jnp.where(place == 0, 0.0, here)
            final = jnp.where(place == last, 0.0, here)
            own = blocks[last - place, pl.ds(0, 64)].astype(f32)
            above = blocks[last - jnp.maximum(place - 1, 0), pl.ds(64, 64)].astype(f32)
            below = blocks[last - jnp.minimum(place + 1, last), pl.ds(64, 64)].astype(f32)
            value = own * here + jnp.where(upper, above * first, below * final)
            out[pl.ds(i * 64, 64), :] = value.astype(bf16)
    send[pl.ds(SLOTS, GRAM), :], send[pl.ds(SLOTS + GRAM, GRAM), :] = halves(grams[...])


def selected(packing, blocks, grams):
    return call(
        select_kernel,
        "select_blocks",
        [array((SLOTS, 128), bf16), array((SENT, 128), bf16)],
        [SMEM, VMEM, VMEM],
        4,
    )(packing, blocks, grams)


def sent_grams(sent):
    return sent[pl.ds(SLOTS, GRAM), :].astype(f32) + sent[pl.ds(SLOTS + GRAM, GRAM), :].astype(f32)


def add_kernel(own, grams, sent, out, out_grams):
    slots = pl.ds(0, SLOTS)
    out[slots, :] = own[slots, :] + sent[slots, :]
    total = grams[...] + sent_grams(sent)
    out_grams[...] = total
    out[pl.ds(SLOTS, GRAM), :], out[pl.ds(SLOTS + GRAM, GRAM), :] = halves(total)


def added(own, grams, sent):
    return call(
        add_kernel,
        "add_sums",
        [array((SENT, 128), bf16), array(grams.shape, f32)],
        [VMEM] * 3,
        4,
    )(own, grams, sent)


def quadratic_forms(patch_gram, total):
    total = total * (1.0 / 5120.0)
    i, j = iota((64, 64), 0), iota((64, 64), 1)
    square = jnp.concatenate([total[:32, :64], total[:32, 64:]], axis=0)
    turned = jnp.transpose(square)
    squares = (
        jnp.where(i > j, 2.0 * square, jnp.where(i == j, square, 0.0)),
        jnp.where(i > j, 2.0 * turned, jnp.where(i == j, total[36:37, :64], 0.0)),
    )
    row, lane = iota((EXT - 64, EXT), 0), iota((EXT - 64, EXT), 1)
    forms = [jnp.concatenate(halves(patch_gram), axis=1)]
    for n, g in enumerate(squares):
        const = total[32 + 2 * n : 33 + 2 * n, :EXT]
        shift = total[33 + 2 * n : 34 + 2 * n, :EXT]
        end = total[33 + 2 * n : 34 + 2 * n, 65:66]
        below = jnp.where(lane < 64, 2.0 * const, jnp.where(lane == 64, const, 0.0))
        linear = jnp.where(lane <= 64, 2.0 * shift, 0.0)
        last = jnp.where(lane == 64, end, 0.0)
        below = jnp.where(row == 0, below, jnp.where(row == 1, linear, 0.0))
        below = jnp.where(row == 2, last, below)
        g = jnp.concatenate([g, jnp.zeros((64, EXT - 64), f32)], axis=1)
        g = jnp.concatenate([g, below], axis=0)
        forms.append(jnp.concatenate(halves(g), axis=1))
    return jnp.concatenate(forms, axis=0)


def total_kernel(patch_gram, own, own_grams, s1, s2, s3, mine, forms):
    slots = pl.ds(0, SLOTS)
    mine[...] = own[slots, :] + s1[slots, :] + s2[slots, :] + s3[slots, :]
    total = own_grams[...] + sent_grams(s1) + sent_grams(s2) + sent_grams(s3)
    forms[...] = quadratic_forms(patch_gram[...], total)


def totals(*args):
    return call(
        total_kernel,
        "total_sums",
        [array((SLOTS, 128), bf16), array((3 * EXT, 2 * EXT), bf16)],
        [VMEM] * 6,
        4,
    )(*args)


def token_rows(x_ref, part, forms, rights, last):
    at = part * 128
    x = jnp.concatenate([x_ref[pl.ds(at, 64), :], x_ref[pl.ds(at + 64, 64), :]], axis=1)
    tail = jnp.where(iota((EXT - 64, 256), 0) == 0, 1.0, 0.0)
    xf = jnp.concatenate([x.astype(f32), tail], axis=0)
    xe = xf.astype(bf16)
    lhs = jnp.transpose(xf).astype(bf16)
    lhs = jnp.concatenate([lhs, lhs], axis=1)
    t = mm(forms[...], jnp.concatenate([xe, xe], axis=0), 1, 0)
    scale = lax.rsqrt(jnp.sum(t[:EXT] * xf, axis=0, keepdims=True) + epsilon)
    row = iota((8, 256), 0)
    stacked = jnp.zeros((8, 256), f32)
    for n in range(2):
        tn = t[(n + 1) * EXT : (n + 2) * EXT]
        squares = (
            scale * scale * jnp.sum(tn * xf, axis=0, keepdims=True)
            + scale * tn[65:66]
            + tn[66:67]
        )
        beta = lax.rsqrt(squares + epsilon)
        stacked = jnp.where(row == 2 * n, scale * beta, stacked)
        stacked = jnp.where(row == 2 * n + 1, beta, stacked)
    columns = jnp.transpose(stacked)
    found = []
    for n, right in enumerate(rights):
        alpha, beta = columns[:, 2 * n : 2 * n + 1], columns[:, 2 * n + 1 : 2 * n + 2]
        value = mm(lhs, right[...], 1, 0) * alpha + beta * last[n : n + 1, :]
        found.append(value.astype(bf16))
    return found


def first_kernel(x_ref, forms, rq, rk, last, q_out, k_out):
    for part in range(2):
        at = pl.ds(part * 256, 256)
        q_out[at, :], k_out[at, :] = token_rows(x_ref, part, forms, (rq, rk), last)


def first_tokens(x, forms, rq, rk, last):
    return call(
        first_kernel, "first_tokens", [array((512, rq.shape[1]), bf16)] * 2, [VMEM] * 5, 6
    )(x, forms, rq, rk, last)


def rest_kernel(
    x_ref, forms, rq, rk, last, q_first, k_first, q_out, k_out, q_buf, k_buf, sems
):
    core = lax.axis_index("tm") % 2
    copies = []

    def send(source, target, at, size):
        at = pl.ds(pl.multiple_of(at, 256), size)
        c = pltpu.make_async_copy(source, target.at[at], sems.at[len(copies)])
        c.start()
        copies.append(c)

    send(q_first, q_out, core * 512, 512)
    send(k_first, k_out, core * 512, 512)
    for part in range(2):
        q_buf[part], k_buf[part] = token_rows(x_ref, part, forms, (rq, rk), last)
        send(q_buf.at[part], q_out, (1 - core) * 512 + part * 256, 256)
        send(k_buf.at[part], k_out, (1 - core) * 512 + part * 256, 256)
    for c in copies:
        c.wait()


def all_tokens(x, forms, rq, rk, last, q_first, k_first):
    width = rq.shape[1]
    return call(
        rest_kernel,
        "rest_tokens",
        [array((1024, width), bf16)] * 2,
        [VMEM] * 7,
        8,
        scratch=[
            pltpu.VMEM((2, 256, width), bf16),
            pltpu.VMEM((2, 256, width), bf16),
            pltpu.SemaphoreType.DMA((6,)),
        ],
        out_specs=[HBM, HBM],
    )(x, forms, rq, rk, last, q_first, k_first)


def in_hbm(x):
    return pltpu.with_memory_space_constraint(x, pltpu.HBM)


def swapped(x, axis, bits):
    return lax.ppermute(x, axis, [(i, i ^ bits) for i in range(lax.axis_size(axis))])


def by_core(x, axis, bits0, bits1):
    route = [(i, i ^ (bits1 if i % 2 else bits0)) for i in range(lax.axis_size(axis))]
    return lax.ppermute(x, axis, route)


def moved(x, axis, by):
    size = lax.axis_size(axis)
    return lax.ppermute(x, axis, [(i, (i + by) % size) for i in range(size)])


def per_device(
    features,
    block_gain,
    conv_weight,
    conv_bias,
    latent_weight,
    latent_bias,
    patch_weight,
    patch_bias,
    shift_mod,
    scale_mod,
    query_weight,
    query_bias,
    query_gain,
    key_weight,
    key_bias,
    key_gain,
    packing,
):
    channels = features.shape[-1]
    row = lambda v: v.reshape(1, -1)
    features, block_gain, conv_bias, lwt, latent_bias, conv_weight = map(
        in_hbm,
        (
            features.reshape(-1, channels),
            block_gain,
            conv_bias,
            latent_weight.T,
            latent_bias,
            conv_weight.reshape(27, channels, channels),
        ),
    )
    ahead, own, act = early_latents(
        features, block_gain, conv_bias, lwt, latent_bias, conv_weight
    )
    before = moved(ahead, "tm", 1)
    own = late_latents(own, act, lwt, conv_weight)
    copies = own_block(own, before)
    copies, patch_weight = lax.optimization_barrier((copies, patch_weight))
    backwards = [list(range(lax.axis_size("rows")))[::-1]]
    plane = lax.all_to_all(copies, "rows", 0, 0, tiled=True, axis_index_groups=backwards)

    rq, rk, last, patch_gram, grams = weights_only(
        patch_weight,
        row(patch_bias),
        row(shift_mod),
        row(scale_mod),
        in_hbm(query_weight),
        in_hbm(key_weight),
        row(query_bias),
        row(key_bias),
        row(query_gain),
        row(key_gain),
    )
    plane, grams = lax.optimization_barrier((plane, grams))
    keep, send = selected(packing, plane, grams)
    own, grams = added(keep, grams, swapped(send, "tm", 1))
    sent = [swapped(own, "tm", bits) for bits in (2, 4, 6)]
    mine, forms = totals(patch_gram, own, grams, *sent)
    first = first_tokens(mine, forms, rq, rk, last)
    return all_tokens(swapped(mine, "tm", 1), forms, rq, rk, last, *first)


def solution(mesh):
    in_specs = (
        P("tm", "rows", None, None),
        P(),
        P(),
        P(),
        P(),
        P(),
        P(),
        P(),
        P(),
        P(),
        P(None, "tm"),
        P("tm"),
        P("tm"),
        P(None, "tm"),
        P("tm"),
        P("tm"),
        P(),
    )
    out_specs = (P("rows", "tm"), P("rows", "tm"))
    return jax.shard_map(
        per_device, mesh=mesh, in_specs=in_specs, out_specs=out_specs, check_vma=False
    )
```

```python
import functools

import jax
import jax.numpy as jnp
from jax import lax
from jax.experimental import pallas as pl
from jax.experimental.pallas import tpu as pltpu
from jax.sharding import PartitionSpec as P

epsilon = 1e-06
bf16 = jnp.bfloat16
f32 = jnp.float32
VMEM = pl.BlockSpec(memory_space=pltpu.VMEM)
SMEM = pl.BlockSpec(memory_space=pltpu.SMEM)
HBM = pl.BlockSpec(memory_space=pltpu.HBM)
MIB = 1 << 20
EXT = 80
GRAM = 48


def mm(a, b, ca, cb):
    return lax.dot_general(a, b, (((ca,), (cb,)), ((), ())), preferred_element_type=f32)


def halves(x):
    high = x.astype(bf16)
    return high, (x - high.astype(f32)).astype(bf16)


def iota(shape, dim):
    return lax.broadcasted_iota(jnp.int32, shape, dim)


def call(kernel, name, out_shape, in_specs, limit, scratch=(), cost=None, **more):
    more.setdefault("out_specs", jax.tree.map(lambda _: VMEM, out_shape))
    return pl.pallas_call(
        kernel,
        out_shape=out_shape,
        in_specs=in_specs,
        scratch_shapes=list(scratch),
        compiler_params=pltpu.CompilerParams(vmem_limit_bytes=limit * MIB),
        cost_estimate=cost,
        name=name,
        **more,
    )


def array(shape, kind):
    return jax.ShapeDtypeStruct(shape, kind)


def folded(lwt, cw, wt, first, count):
    for k in range(first, first + count):
        high, low = halves(mm(lwt, cw[k], 1, 1))
        at = (k // 9) * 288 + (k % 9) * 16
        wt[pl.ds(at, 16), :] = high
        wt[pl.ds(at + 144, 16), :] = low


def shifted_sum(by_e):
    lane = iota((16, 128), 1)
    left = jnp.where(lane == 0, 0.0, pltpu.roll(by_e[0], 1, 1))
    right = jnp.where(lane == 127, 0.0, pltpu.roll(by_e[2], 127, 1))
    return left + by_e[1] + right


def contributions(gts, fo, ro):
    by_e = []
    for e in range(3):
        total = None
        for f in range(2):
            for r in range(2):
                a, b = f + 2 - fo, r + 2 - ro
                if a not in gts or not 0 <= b < 3:
                    continue
                k, q = b * 3 + e, f * 2 + r
                part = (
                    gts[a][pl.ds(k * 16, 16), pl.ds(q * 128, 128)]
                    + gts[a][pl.ds(144 + k * 16, 16), pl.ds(q * 128, 128)]
                )
                total = part if total is None else total + part
        by_e.append(total)
    return shifted_sum(by_e)


def chunks_of(source, target, sems, start, count, size, first_sem):
    return [
        pltpu.make_async_copy(
            source.at[pl.ds(start + i * size, size)],
            target.at[pl.ds(i * size, size)],
            sems.at[first_sem + i],
        )
        for i in range(count)
    ]


def silu_normed(values, gain):
    mean = jnp.mean(values * values, axis=-1, keepdims=True)
    y = values * lax.rsqrt(mean + epsilon) * gain
    return (y / (1.0 + jnp.exp(-y))).astype(bf16)


def early_kernel(
    feat_hbm, gain_hbm, bias_hbm, lwt_hbm, lb_hbm, cw_hbm, ahead, own, act_out,
    feat, gain, bias, lwt_ref, lb, cw, wt, gt, sems,
):
    small = [
        pltpu.make_async_copy(a, b, sems.at[6 + i])
        for i, (a, b) in enumerate(
            (
                (feat_hbm, feat),
                (gain_hbm, gain),
                (bias_hbm, bias),
                (lwt_hbm, lwt_ref),
                (lb_hbm, lb),
            )
        )
    ]
    for c in small:
        c.start()
    copies = chunks_of(cw_hbm, cw, sems, 0, 3, 6, 0)
    for c in copies:
        c.start()
    for c in small:
        c.wait()
    lwt = lwt_ref[...]
    act_out[...] = silu_normed(feat[...].astype(f32), gain[...].reshape(1, -1))
    for i, c in enumerate(copies):
        c.wait()
        folded(lwt, cw, wt, i * 6, 6)
    gt[pl.ds(0, 288), :] = mm(wt[pl.ds(0, 288), :], act_out[...], 1, 1)
    direct = mm(lwt, feat[...], 1, 1)
    const = jnp.sum(lwt.astype(f32) * bias[...].reshape(1, -1), axis=1, keepdims=True)
    const = const + jnp.transpose(lb[...].reshape(1, -1))
    gt[pl.ds(288, 288), :] = mm(wt[pl.ds(288, 288), :], act_out[...], 1, 1)
    gt0, gt1 = gt.at[pl.ds(0, 288)], gt.at[pl.ds(288, 288)]
    for ro in range(4):
        for fo in (2, 3):
            ahead[fo - 2, ro] = contributions({0: gt0, 1: gt1}, fo, ro).astype(bf16)
        own[0, ro] = jnp.zeros((16, 128), f32)
        own[1, ro] = contributions({1: gt1}, 1, ro)
        if 1 <= ro < 3:
            for fo in range(2):
                q = fo * 2 + ro - 1
                own[fo, ro] += direct[:, q * 128 : (q + 1) * 128] + const


def early_latents(*args):
    return call(
        early_kernel,
        "early_latents",
        [array((2, 4, 16, 128), bf16), array((2, 4, 16, 128), f32), array((512, 384), bf16)],
        [HBM] * 6,
        20,
        scratch=[
            pltpu.VMEM((512, 384), bf16),
            pltpu.VMEM((384,), f32),
            pltpu.VMEM((384,), f32),
            pltpu.VMEM((16, 384), bf16),
            pltpu.VMEM((16,), f32),
            pltpu.VMEM((18, 384, 384), bf16),
            pltpu.VMEM((576, 384), bf16),
            pltpu.VMEM((576, 512), f32),
            pltpu.SemaphoreType.DMA((11,)),
        ],
    )(*args)


def late_kernel(own, act, lwt_hbm, cw_hbm, out, lwt, cw, wt, gt, sems):
    small = pltpu.make_async_copy(lwt_hbm, lwt, sems.at[3])
    small.start()
    copies = chunks_of(cw_hbm, cw, sems, 18, 3, 3, 0)
    for c in copies:
        c.start()
    small.wait()
    for i, c in enumerate(copies):
        c.wait()
        folded(lwt[...], cw, wt, i * 3, 3)
    gt[...] = mm(wt[...], act[...], 1, 1)
    for fo in range(2):
        for ro in range(4):
            out[fo, ro] = own[fo, ro] + contributions({2: gt}, fo, ro)


def late_latents(*args):
    return call(
        late_kernel,
        "late_latents",
        array((2, 4, 16, 128), f32),
        [VMEM] * 2 + [HBM] * 2,
        10,
        scratch=[
            pltpu.VMEM((16, 384), bf16),
            pltpu.VMEM((9, 384, 384), bf16),
            pltpu.VMEM((288, 384), bf16),
            pltpu.VMEM((288, 512), f32),
            pltpu.SemaphoreType.DMA((4,)),
        ],
        cost=pl.CostEstimate(flops=3 * 10**9, bytes_accessed=5 * 10**6, transcendentals=0),
    )(*args)


def weights_kernel(
    pw, pb, shift, scale, wq_hbm, wk_hbm, bq, bk, gq, gk,
    rq, rk, last, patch_gram, grams, wq, wk, parts, sems,
):
    width = pw.shape[1]
    chunk = width // 4
    copies = chunks_of(wq_hbm, wq, sems, 0, 4, chunk, 0)
    copies = copies + chunks_of(wk_hbm, wk, sems, 0, 4, chunk, 4)
    for c in copies[:3]:
        c.start()
    to, at = iota((64, 64), 0), iota((64, 64), 1)
    wanted = 4 * (to % 16) + 2 * ((to // 16) % 2) + to // 32
    order = jnp.where(at == wanted, 1.0, 0.0).astype(bf16)
    rows = mm(order, pw[...], 1, 0)
    rows = rows - jnp.mean(rows, axis=1, keepdims=True)
    const = pb[...] - jnp.mean(pb[...], axis=1, keepdims=True)
    const_tail = jnp.where(iota((16, width), 0) == 0, const, 0.0)
    centered = jnp.concatenate([rows, const_tail], axis=0)
    high, low = halves(centered)
    both = mm(jnp.concatenate([high, low], axis=0), high, 1, 1)
    cross = both[EXT:, :]
    patch_gram[...] = (both[:EXT, :] + cross + jnp.transpose(cross)) * (1.0 / width)
    scaled = centered * (1.0 + scale[...])
    high, low = halves(jnp.where(iota((EXT, width), 0) == 65, shift[...], scaled))
    parts[pl.ds(0, EXT), :] = high
    parts[pl.ds(EXT, EXT), :] = low
    found = []
    for n, (w, bias, gain, right) in enumerate(((wq, bq, gq, rq), (wk, bk, gk, rk))):
        both = None
        for i in range(4):
            copies[n * 4 + i].wait()
            if n * 4 + i + 3 < 8:
                copies[n * 4 + i + 3].start()
            at = pl.ds(i * chunk, chunk)
            part = mm(parts[:, at], w[at, :], 1, 0)
            both = part if both is None else both + part
        rows = both[:EXT, :] + both[EXT:, :]
        rows = rows + jnp.where(iota(rows.shape, 0) == 65, bias[...], 0.0)
        high, low = halves(rows)
        pairs = mm(jnp.concatenate([high, low], axis=0), high, 1, 1)
        cross = pairs[EXT:, :]
        found.append(pairs[:EXT, :] + cross + jnp.transpose(cross))
        rows = rows * gain[...]
        shifted = iota(rows.shape, 0) == 65
        high, low = halves(jnp.where(shifted, 0.0, rows))
        right[pl.ds(0, EXT), :] = high
        right[pl.ds(EXT, EXT), :] = low
        last[n : n + 1, :] = jnp.sum(jnp.where(shifted, rows, 0.0), axis=0, keepdims=True)
    i, j = iota((EXT, EXT), 0), iota((EXT, EXT), 1)
    square = jnp.where(i >= j, found[0], found[1])
    grams[pl.ds(0, 32), :] = jnp.concatenate([square[:32, :64], square[32:64, :64]], axis=1)
    grams[pl.ds(32, 16), :] = jnp.zeros((16, 128), f32)
    grams[pl.ds(32, 2), pl.ds(0, EXT)] = found[0][64:66]
    grams[pl.ds(34, 2), pl.ds(0, EXT)] = found[1][64:66]
    diagonal = jnp.sum(jnp.where(i == j, found[1], 0.0), axis=0, keepdims=True)
    grams[pl.ds(36, 1), pl.ds(0, EXT)] = diagonal


def weights_only(pw, pb, shift, scale, wq, wk, bq, bk, gq, gk):
    width, part = wq.shape
    return call(
        weights_kernel,
        "weights_only",
        [
            array((2 * EXT, part), bf16),
            array((2 * EXT, part), bf16),
            array((8, part), f32),
            array((EXT, EXT), f32),
            array((GRAM, 128), f32),
        ],
        [VMEM] * 4 + [HBM] * 2 + [VMEM] * 4,
        36,
        scratch=[
            pltpu.VMEM((width, part), bf16),
            pltpu.VMEM((width, part), bf16),
            pltpu.VMEM((2 * EXT, width), bf16),
            pltpu.SemaphoreType.DMA((8,)),
        ],
        cost=pl.CostEstimate(
            flops=4 * 2 * EXT * width * part * 4, bytes_accessed=2 * width * part * 2, transcendentals=0
        ),
    )(pw, pb, shift, scale, wq, wk, bq, bk, gq, gk)


def block_kernel(own, before, out):
    first = jnp.where(lax.axis_index("tm") == 0, 0.0, 1.0)
    rows = []
    for ro in (1, 2, 3, 0):
        frames = [own[f, ro] + before[f, ro].astype(f32) * first for f in range(2)]
        rows.append(jnp.concatenate(frames, axis=1).astype(bf16))
    source, target = iota((256, 256), 0), iota((256, 256), 1)
    wanted = ((target // 64) % 2) * 128 + 2 * (target % 64) + target // 128
    pick = jnp.where(source == wanted, 1.0, 0.0).astype(bf16)
    spread = mm(jnp.concatenate(rows, axis=0), pick, 1, 0).astype(bf16)
    block = jnp.concatenate(
        [spread[:32, :128], spread[:32, 128:], spread[32:, :128], spread[32:, 128:]], axis=0
    )
    for i in range(out.shape[0]):
        out[i] = block


def own_block(own, before):
    return call(
        block_kernel, "own_block", array((lax.axis_size("rows"), 128, 128), bf16), [VMEM] * 2, 4
    )(own, before)


SLOTS = 256
SENT = SLOTS + 2 * GRAM


def select_kernel(packing, blocks, grams, keep, send):
    t, r = lax.axis_index("tm"), lax.axis_index("rows")
    last = blocks.shape[0] - 1
    core = t % 2
    upper = (iota((64, 128), 0) // 16) % 2 == 0
    for out, half in ((keep, core), (send, 1 - core)):
        for i in range(4):
            ident = packing[r * 8 + half * 4 + i]
            place = ident % 16
            here = jnp.where(ident // 16 == t, 1.0, 0.0)
            first = jnp.where(place == 0, 0.0, here)
            final = jnp.where(place == last, 0.0, here)
            own = blocks[last - place, pl.ds(0, 64)].astype(f32)
            above = blocks[last - jnp.maximum(place - 1, 0), pl.ds(64, 64)].astype(f32)
            below = blocks[last - jnp.minimum(place + 1, last), pl.ds(64, 64)].astype(f32)
            value = own * here + jnp.where(upper, above * first, below * final)
            out[pl.ds(i * 64, 64), :] = value.astype(bf16)
    send[pl.ds(SLOTS, GRAM), :], send[pl.ds(SLOTS + GRAM, GRAM), :] = halves(grams[...])


def selected(packing, blocks, grams):
    return call(
        select_kernel,
        "select_blocks",
        [array((SLOTS, 128), bf16), array((SENT, 128), bf16)],
        [SMEM, VMEM, VMEM],
        4,
    )(packing, blocks, grams)


def sent_grams(sent):
    return sent[pl.ds(SLOTS, GRAM), :].astype(f32) + sent[pl.ds(SLOTS + GRAM, GRAM), :].astype(f32)


def add_kernel(own, grams, sent, out, out_grams):
    slots = pl.ds(0, SLOTS)
    out[slots, :] = own[slots, :] + sent[slots, :]
    total = grams[...] + sent_grams(sent)
    out_grams[...] = total
    out[pl.ds(SLOTS, GRAM), :], out[pl.ds(SLOTS + GRAM, GRAM), :] = halves(total)


def added(own, grams, sent):
    return call(
        add_kernel,
        "add_sums",
        [array((SENT, 128), bf16), array(grams.shape, f32)],
        [VMEM] * 3,
        4,
    )(own, grams, sent)


def quadratic_forms(patch_gram, total):
    total = total * (1.0 / 5120.0)
    i, j = iota((64, 64), 0), iota((64, 64), 1)
    square = jnp.concatenate([total[:32, :64], total[:32, 64:]], axis=0)
    turned = jnp.transpose(square)
    squares = (
        jnp.where(i > j, 2.0 * square, jnp.where(i == j, square, 0.0)),
        jnp.where(i > j, 2.0 * turned, jnp.where(i == j, total[36:37, :64], 0.0)),
    )
    row, lane = iota((EXT - 64, EXT), 0), iota((EXT - 64, EXT), 1)
    forms = [jnp.concatenate(halves(patch_gram), axis=1)]
    for n, g in enumerate(squares):
        const = total[32 + 2 * n : 33 + 2 * n, :EXT]
        shift = total[33 + 2 * n : 34 + 2 * n, :EXT]
        end = total[33 + 2 * n : 34 + 2 * n, 65:66]
        below = jnp.where(lane < 64, 2.0 * const, jnp.where(lane == 64, const, 0.0))
        linear = jnp.where(lane <= 64, 2.0 * shift, 0.0)
        last = jnp.where(lane == 64, end, 0.0)
        below = jnp.where(row == 0, below, jnp.where(row == 1, linear, 0.0))
        below = jnp.where(row == 2, last, below)
        g = jnp.concatenate([g, jnp.zeros((64, EXT - 64), f32)], axis=1)
        g = jnp.concatenate([g, below], axis=0)
        forms.append(jnp.concatenate(halves(g), axis=1))
    return jnp.concatenate(forms, axis=0)


def total_kernel(patch_gram, own, own_grams, s1, s2, s3, mine, forms):
    slots = pl.ds(0, SLOTS)
    mine[...] = own[slots, :] + s1[slots, :] + s2[slots, :] + s3[slots, :]
    total = own_grams[...] + sent_grams(s1) + sent_grams(s2) + sent_grams(s3)
    forms[...] = quadratic_forms(patch_gram[...], total)


def totals(*args):
    return call(
        total_kernel,
        "total_sums",
        [array((SLOTS, 128), bf16), array((3 * EXT, 2 * EXT), bf16)],
        [VMEM] * 6,
        4,
    )(*args)


def token_rows(x_ref, slots, forms, rights, last):
    x = jnp.concatenate([x_ref[pl.ds(i * 64, 64), :] for i in slots], axis=1)
    count = x.shape[1]
    tail = jnp.where(iota((EXT - 64, count), 0) == 0, 1.0, 0.0)
    xf = jnp.concatenate([x.astype(f32), tail], axis=0)
    xe = xf.astype(bf16)
    lhs = jnp.transpose(xf).astype(bf16)
    lhs = jnp.concatenate([lhs, lhs], axis=1)
    t = mm(forms[...], jnp.concatenate([xe, xe], axis=0), 1, 0)
    scale = lax.rsqrt(jnp.sum(t[:EXT] * xf, axis=0, keepdims=True) + epsilon)
    row = iota((8, count), 0)
    stacked = jnp.zeros((8, count), f32)
    for n in range(2):
        tn = t[(n + 1) * EXT : (n + 2) * EXT]
        squares = (
            scale * scale * jnp.sum(tn * xf, axis=0, keepdims=True)
            + scale * tn[65:66]
            + tn[66:67]
        )
        beta = lax.rsqrt(squares + epsilon)
        stacked = jnp.where(row == 2 * n, scale * beta, stacked)
        stacked = jnp.where(row == 2 * n + 1, beta, stacked)
    columns = jnp.transpose(stacked)
    found = []
    for n, right in enumerate(rights):
        alpha, beta = columns[:, 2 * n : 2 * n + 1], columns[:, 2 * n + 1 : 2 * n + 2]
        value = mm(lhs, right[...], 1, 0) * alpha + beta * last[n : n + 1, :]
        found.append(value.astype(bf16))
    return found


def first_kernel(x_ref, forms, rq, rk, last, q_out, k_out):
    q_out[...], k_out[...] = token_rows(x_ref, range(4), forms, (rq, rk), last)


def first_tokens(x, forms, rq, rk, last):
    return call(
        first_kernel, "first_tokens", [array((512, rq.shape[1]), bf16)] * 2, [VMEM] * 5, 6
    )(x, forms, rq, rk, last)


def rest_kernel(
    x_ref, forms, rq, rk, last, q_first, k_first, q_out, k_out, q_buf, k_buf, sems
):
    core = lax.axis_index("tm") % 2
    copies = []

    def send(source, target, at, size):
        at = pl.ds(pl.multiple_of(at, 256), size)
        c = pltpu.make_async_copy(source, target.at[at], sems.at[len(copies)])
        c.start()
        copies.append(c)

    send(q_first, q_out, core * 512, 512)
    send(k_first, k_out, core * 512, 512)
    for part in range(2):
        q_buf[part], k_buf[part] = token_rows(x_ref, (2 * part, 2 * part + 1), forms, (rq, rk), last)
        send(q_buf.at[part], q_out, (1 - core) * 512 + part * 256, 256)
        send(k_buf.at[part], k_out, (1 - core) * 512 + part * 256, 256)
    for c in copies:
        c.wait()


def all_tokens(x, forms, rq, rk, last, q_first, k_first):
    width = rq.shape[1]
    return call(
        rest_kernel,
        "rest_tokens",
        [array((1024, width), bf16)] * 2,
        [VMEM] * 7,
        8,
        scratch=[
            pltpu.VMEM((2, 256, width), bf16),
            pltpu.VMEM((2, 256, width), bf16),
            pltpu.SemaphoreType.DMA((6,)),
        ],
        out_specs=[HBM, HBM],
    )(x, forms, rq, rk, last, q_first, k_first)


def in_hbm(x):
    return pltpu.with_memory_space_constraint(x, pltpu.HBM)


def swapped(x, axis, bits):
    return lax.ppermute(x, axis, [(i, i ^ bits) for i in range(lax.axis_size(axis))])


def by_core(x, axis, bits0, bits1):
    route = [(i, i ^ (bits1 if i % 2 else bits0)) for i in range(lax.axis_size(axis))]
    return lax.ppermute(x, axis, route)


def moved(x, axis, by):
    size = lax.axis_size(axis)
    return lax.ppermute(x, axis, [(i, (i + by) % size) for i in range(size)])


def per_device(
    features,
    block_gain,
    conv_weight,
    conv_bias,
    latent_weight,
    latent_bias,
    patch_weight,
    patch_bias,
    shift_mod,
    scale_mod,
    query_weight,
    query_bias,
    query_gain,
    key_weight,
    key_bias,
    key_gain,
    packing,
):
    channels = features.shape[-1]
    row = lambda v: v.reshape(1, -1)
    features, block_gain, conv_bias, lwt, latent_bias, conv_weight = map(
        in_hbm,
        (
            features.reshape(-1, channels),
            block_gain,
            conv_bias,
            latent_weight.T,
            latent_bias,
            conv_weight.reshape(27, channels, channels),
        ),
    )
    ahead, own, act = early_latents(
        features, block_gain, conv_bias, lwt, latent_bias, conv_weight
    )
    before = moved(ahead, "tm", 1)
    own = late_latents(own, act, lwt, conv_weight)
    copies = own_block(own, before)
    copies, patch_weight = lax.optimization_barrier((copies, patch_weight))
    backwards = [list(range(lax.axis_size("rows")))[::-1]]
    plane = lax.all_to_all(copies, "rows", 0, 0, tiled=True, axis_index_groups=backwards)

    rq, rk, last, patch_gram, grams = weights_only(
        patch_weight,
        row(patch_bias),
        row(shift_mod),
        row(scale_mod),
        in_hbm(query_weight),
        in_hbm(key_weight),
        row(query_bias),
        row(key_bias),
        row(query_gain),
        row(key_gain),
    )
    plane, grams = lax.optimization_barrier((plane, grams))
    keep, send = selected(packing, plane, grams)
    own, grams = added(keep, grams, swapped(send, "tm", 1))
    sent = [by_core(own, "tm", 2, 6), swapped(own, "tm", 4), by_core(own, "tm", 6, 2)]
    mine, forms = totals(patch_gram, own, grams, *sent)
    first = first_tokens(mine, forms, rq, rk, last)
    return all_tokens(swapped(mine, "tm", 1), forms, rq, rk, last, *first)


def solution(mesh):
    in_specs = (
        P("tm", "rows", None, None),
        P(),
        P(),
        P(),
        P(),
        P(),
        P(),
        P(),
        P(),
        P(),
        P(None, "tm"),
        P("tm"),
        P("tm"),
        P(None, "tm"),
        P("tm"),
        P("tm"),
        P(),
    )
    out_specs = (P("rows", "tm"), P("rows", "tm"))
    return jax.shard_map(
        per_device, mesh=mesh, in_specs=in_specs, out_specs=out_specs, check_vma=False
    )
```
